128 devices in a mesh: sec: 2 (over z_lo), row: 8 (over x, z_hi), col: 8 (over y, core).
Axes of the slice: x: 4, y: 4, z: 4 (z_hi: 2, z_lo: 2; z = z_hi * 2 + z_lo), core: 2. Of those that a mesh axis runs over, the one named last changes fastest.
Arguments:
- held_inverse: bfloat16 [12288, 12288], P('row', ('sec', 'col')), as said below
- factor_panels: bfloat16 [2, 12288, 1024], P(None, ('sec', 'col'), 'row'), may hold values from -0.125 to 0.125
- block_inverses: bfloat16 [2, 1024, 1024], P(None, 'row'), as said below
- covariance: float32 [12288, 12288], P('row', ('sec', 'col')), may hold values from -0.9 to 0.9
Outputs:
- updated: float32 [12288, 12288], P('row', ('sec', 'col'))
The draws below stay inside these ranges and needn't reach their ends.
Inputs may be any that keep to these rules, and one draw needn't show every extreme that they name: held_inverse is lower triangular with a positive diagonal. Each block of block_inverses is lower triangular with a positive diagonal.
All inputs are finite; a program needn't handle non-finite values.
Results may differ from the reference program's by a relative error of at most 0.0038.
Values may be sent and summed in bfloat16 or wider, within the bound.
A program may use at most 128 MiB of HBM per device.

```python
import jax
import jax.numpy as jnp
from jax import lax

M = 12288
B = 1024
PANELS = 2


def draw_held_inverse(key, part):
    first, second = jax.random.split(jax.random.fold_in(key, 11), 2)
    lower = jax.random.normal(first, (M, M), jnp.float32) * (1.5 / jnp.sqrt(M * 1.0))
    diagonal = jax.random.uniform(second, (M,), jnp.float32, 0.6, 1.6)
    return (jnp.tril(lower, -1) + jnp.diag(diagonal)).astype(jnp.bfloat16)


def draw_block_inverses(key, part):
    first, second = jax.random.split(jax.random.fold_in(key, 23))
    lower = jax.random.normal(first, (PANELS, B, B), jnp.float32) / jnp.sqrt(B * 1.0)
    diagonal = jax.random.uniform(second, (PANELS, B), jnp.float32, 0.5, 2.0)
    eye = jnp.eye(B, dtype=jnp.float32)
    return (jnp.tril(lower, -1) + diagonal[:, :, None] * eye[None]).astype(jnp.bfloat16)


def levels(rng, extent, shards, low, top_value):
    level, own = 1.0, jax.random.fold_in(rng, 6)
    for position, parts in shards:
        steps = jnp.exp(jax.random.uniform(jax.random.fold_in(own, position), (parts,), jnp.float32, low / len(shards), top_value / len(shards)))
        level = level * jnp.repeat(steps, extent[position] // parts).reshape([-1 if axis == position else 1 for axis in range(len(extent))])
    return level


def normal_values(rng, shape, scale, limit, pieces=(), kind=jnp.bfloat16):
    array = jax.random.normal(rng, shape, jnp.float32) * scale
    if len(pieces) > 0:
        array = levels(rng, shape, pieces, -0.22, 0.18) * array
    return jnp.clip(array, min=-limit, max=limit).astype(kind)


def setup_inputs(seed: int = 0) -> dict:
    arg_keys = jax.random.split(jax.random.key(seed), 5)
    held_inverse = draw_held_inverse(jax.random.fold_in(arg_keys[4], 71), 0)
    factor_panels = normal_values(arg_keys[1], (PANELS, M, B), (B * PANELS) ** -0.5, 0.125, ((1, 16), (2, 8)))
    block_inverses = draw_block_inverses(jax.random.fold_in(arg_keys[4], 71), 0)
    covariance = normal_values(arg_keys[3], (M, M), 0.15, 0.9, ((0, 8), (1, 16)), jnp.float32)
    return {"held_inverse": held_inverse, "factor_panels": factor_panels, "block_inverses": block_inverses, "covariance": covariance}


def reference(held_inverse, factor_panels, block_inverses, covariance):
    total = covariance
    for panel in range(PANELS):
        scaled = jnp.dot(factor_panels[panel], block_inverses[panel], preferred_element_type=jnp.float32).astype(jnp.bfloat16)
        inverse = (-jnp.dot(held_inverse, scaled, preferred_element_type=jnp.float32)).astype(jnp.bfloat16)
        total = total + lax.dot_general(inverse, inverse, (((1,), (1,)), ((), ())), preferred_element_type=jnp.float32)
    return total
```

```python
import jax
import jax.numpy as jnp
from jax import lax
from jax.experimental import pallas as pl
from jax.experimental.pallas import tpu as pltpu
from jax.sharding import Mesh
from jax.sharding import PartitionSpec as P

MESH = pl.DeviceIdType.MESH
AXES = ("zl", "x", "zh", "y", "k")
BF16 = jnp.bfloat16
F32 = jnp.float32

CHUNKS = 4
SPREAD = 3


def al(i, n):
    return pl.multiple_of(i, n)


def kernel(
    l_ref, f_ref, d_ref, c_ref, out_ref,
    lb, g, db, s, t, own, rs1, rs2, rsz, ir, iq, cb, send, recv, local,
):
    zl, x, zh, y, k = (lax.axis_index(a) for a in AXES)
    rows, cols = l_ref.shape
    _, _, fcols = f_ref.shape
    drows, width = d_ref.shape[1:]
    wide = width // CHUNKS
    part = rows // 8
    pair = 2 * part
    r = 2 * x + zh
    xp, xm = lax.rem(x + 1, 4), lax.rem(x + 3, 4)
    yp, ym, y2 = lax.rem(y + 1, 4), lax.rem(y + 3, 4), lax.rem(y + 2, 4)
    piece = 2 * y + zl

    ys, zs = 2 * lax.rem(x, 2) + zh, x // 2
    d_to, e_to = lax.rem(y - ys + 4, 4), lax.rem(zl + zs, 2)
    tr_to = {"zl": zs, "x": lax.rem(x + d_to, 4), "zh": lax.rem(zh + e_to, 2), "y": ys}
    xs, hs = 2 * zl + y // 2, lax.rem(y, 2)
    d_from, e_from = lax.rem(x - xs + 4, 4), lax.rem(zh + hs, 2)
    tr_from = {"zl": lax.rem(zl + e_from, 2), "x": xs, "zh": hs, "y": lax.rem(y + d_from, 4)}
    diagonal = jnp.logical_and(d_to == 0, e_to == 0)
    got = 2 * lax.rem(y + d_from, 4) + lax.rem(zl + e_from, 2)
    gotz = 2 * lax.rem(y + d_from, 4) + lax.rem(zl + e_from + 1, 2)
    bx = lax.rem(y + d_from, 4)
    bxp, bxm = lax.rem(bx + 1, 4), lax.rem(bx + 3, 4)

    group = [
        {"x": lax.rem(x + dx, 4), "zh": lax.rem(zh + dz, 2)}
        for dx in range(4) for dz in range(2) if dx or dz
    ]
    peers = group + [
        {"k": 1 - k}, {"zh": 1 - zh, "k": 1 - k}, {"x": xp, "k": 1 - k}, {"x": xm, "k": 1 - k},
        {"zl": 1 - zl}, {"y": yp}, {"y": ym},
    ]
    barrier = pltpu.get_barrier_semaphore()
    for peer in peers:
        pl.semaphore_signal(barrier, inc=1, device_id=peer, device_id_type=MESH)

    @pl.when(jnp.logical_not(diagonal))
    def _():
        pl.semaphore_signal(barrier, inc=1, device_id=tr_to, device_id_type=MESH)
        pl.semaphore_signal(barrier, inc=1, device_id=tr_from, device_id_type=MESH)
        pl.semaphore_wait(barrier, len(peers) + 2)

    @pl.when(diagonal)
    def _():
        pl.semaphore_wait(barrier, len(peers))

    counts = {"remote": 0, "local": 0}
    sent = []

    def remote(src, dst, device):
        n = counts["remote"]
        counts["remote"] += 1
        copy = pltpu.make_async_remote_copy(
            src_ref=src, dst_ref=dst, send_sem=send.at[n], recv_sem=recv.at[n],
            device_id=device, device_id_type=MESH,
        )
        sent.append(copy)
        copy.start()
        return copy

    def here(src, dst):
        n = counts["local"]
        counts["local"] += 1
        copy = pltpu.make_async_copy(src, dst, local.at[n])
        copy.start()
        return copy

    def at_f(xx, kk, hh):
        return g.at[xx, pl.ds(al(kk * cols, cols), cols), pl.ds(al(hh * fcols, fcols), fcols)]

    mine = f_ref.at[k]
    other = f_ref.at[1 - k]
    slot = at_f(x, k, zh)
    f_own = here(mine, slot)
    f_z = [remote(mine, slot, {"zh": 1 - zh}), remote(other, slot, {"zh": 1 - zh, "k": 1 - k})]
    f_k = remote(other, slot, {"k": 1 - k})
    f_x = [
        remote(mine, slot, {"x": xp}), remote(other, slot, {"x": xp, "k": 1 - k}),
        remote(mine, slot, {"x": xm}), remote(other, slot, {"x": xm, "k": 1 - k}),
    ]
    dpart = drows // 8
    dsrc = d_ref.at[k, pl.ds(al(piece * dpart, dpart), dpart), :]
    d_own = here(dsrc, db.at[r, piece])
    d_r = [remote(dsrc, db.at[r, piece], peer) for peer in group]
    l_own = here(l_ref, lb.at[k])
    l_k = remote(l_ref, lb.at[k], {"k": 1 - k})
    c_own = here(c_ref, cb)

    d_own.wait()
    for copy in d_r:
        copy.wait_recv()
    d_z = remote(db.at[:, piece], db.at[:, piece], {"zl": 1 - zl})
    for copy in f_z:
        copy.wait_recv()
    ahead = g.at[x, :, pl.ds(al((1 - zh) * fcols, fcols), fcols)]
    f_x2 = [remote(ahead, ahead, {"x": xp}), remote(ahead, ahead, {"x": xm})]
    d_z.wait_recv()
    two = db.at[:, pl.ds(2 * y, 2)]
    d_y = [remote(two, two, {"y": yp}), remote(two, two, {"y": ym})]
    for copy in f_x + f_x2:
        copy.wait_recv()
    low, high = g.at[xm, pl.ds(0, cols)], g.at[xp, pl.ds(cols, cols)]
    f_x3 = [remote(low, low, {"x": xp}), remote(high, high, {"x": xm})]
    for copy in d_y:
        copy.wait_recv()
    low, high = db.at[:, 2 * ym], db.at[:, 2 * yp + 1]
    d_y2 = [remote(low, low, {"y": yp}), remote(high, high, {"y": ym})]
    f_own.wait()
    f_k.wait_recv()
    l_own.wait()
    l_k.wait_recv()
    for copy in d_y2 + f_x3:
        copy.wait_recv()

    block = 512
    steps = rows // block
    done = {}

    def slab(b):
        return pl.ds(al(b * pair, pair), pair)

    def thin(p):
        return pl.ds(al(p * part, part), part)

    def s1(c):
        lanes = slice(c * wide, (c + 1) * wide)
        first = c * wide // (2 * drows)

        @pl.loop(0, steps)
        def _(i):
            m = pl.ds(al(i * block, block), block)
            acc = None
            for xx in range(first, 4):
                rhs = db[2 * xx : 2 * xx + 2, :, :, lanes].reshape(2 * drows, wide)
                term = jnp.dot(g[xx, m, :], rhs, preferred_element_type=F32)
                acc = term if acc is None else acc + term
            s[m, :] = acc.astype(BF16)

        @pl.loop(0, steps)
        def _(i):
            m = pl.ds(al(i * block, block), block)
            acc = jnp.dot(lb[0, m, :], s[:cols, :], preferred_element_type=F32)
            acc += jnp.dot(lb[1, m, :], s[cols:, :], preferred_element_type=F32)
            t[c, m, :] = acc.astype(BF16)

        done["rs1", c] = [
            remote(t.at[c, thin(2 * y2)], rs1.at[c, 0], {"y": yp}),
            remote(t.at[c, thin(2 * y2 + 1)], rs1.at[c, 1], {"y": ym}),
        ]

    def s2(c):
        up, down = done["rs1", c]
        up.wait_recv()
        t[c, thin(2 * yp), :] = (t[c, thin(2 * yp), :].astype(F32) + rs1[c, 0].astype(F32)).astype(BF16)
        down.wait_recv()
        t[c, thin(2 * ym + 1), :] = (t[c, thin(2 * ym + 1), :].astype(F32) + rs1[c, 1].astype(F32)).astype(BF16)
        done["rs2", c] = [
            remote(t.at[c, slab(yp)], rs2.at[c, 0], {"y": yp}),
            remote(t.at[c, slab(ym)], rs2.at[c, 1], {"y": ym}),
        ]

    def s3(c):
        for copy in done["rs2", c]:
            copy.wait_recv()
        away = 1 - zl
        for dst, z in ((rsz.at[c, 0], away), (own.at[c], zl)):
            total = t[c, thin(2 * y + z), :].astype(F32)
            for side in range(2):
                total += rs2[c, side, pl.ds(al(z * part, part), part), :].astype(F32)
            dst[...] = total.astype(dst.dtype)
        done["rsz", c] = remote(rsz.at[c, 0], rsz.at[c, 1], {"zl": 1 - zl})

    def s4(c):
        done["rsz", c].wait_recv()
        ir[k, c, thin(piece), :] = (-(own[c] + rsz[c, 1].astype(F32))).astype(BF16)
        src = ir.at[k, c, thin(piece)]
        done["agz", c] = remote(src, src, {"zl": 1 - zl})
        n = counts["remote"]
        counts["remote"] += 1
        dst = iq.at[k, c, thin(piece)]
        away = pltpu.make_async_remote_copy(
            src_ref=src, dst_ref=dst, send_sem=send.at[n], recv_sem=recv.at[n], device_id=tr_to, device_id_type=MESH
        )
        still = pltpu.make_async_copy(src, dst, recv.at[n])
        done["tr", c] = away, still

        @pl.when(jnp.logical_not(diagonal))
        def _():
            away.start()

        @pl.when(diagonal)
        def _():
            still.start()

    def s5(c):
        done["agz", c].wait_recv()
        src = ir.at[k, c, slab(y)]
        done["agy", c] = [remote(src, src, {"y": yp}), remote(src, src, {"y": ym})]
        away, still = done["tr", c]

        @pl.when(jnp.logical_not(diagonal))
        def _():
            away.wait_recv()

        @pl.when(diagonal)
        def _():
            still.wait()

        src = iq.at[k, c, thin(got)]
        done["cgz", c] = remote(src, src, {"zh": 1 - zh})

    def s6(c):
        for copy in done["agy", c]:
            copy.wait_recv()
        low, high = ir.at[k, c, thin(2 * ym)], ir.at[k, c, thin(2 * yp + 1)]
        done["agy2", c] = [remote(low, low, {"y": yp}), remote(high, high, {"y": ym})]
        done["cgz", c].wait_recv()
        src = iq.at[k, c, slab(bx)]
        done["cgx", c] = [remote(src, src, {"x": xp}), remote(src, src, {"x": xm})]

    def s7(c):
        for copy in done["agy2", c]:
            copy.wait_recv()
        done["ir", c] = remote(ir.at[k, c], ir.at[k, c], {"k": 1 - k})
        for copy in done["cgx", c]:
            copy.wait_recv()
        low, high = iq.at[k, c, thin(2 * bxm)], iq.at[k, c, thin(2 * bxp + 1)]
        done["cgx2", c] = [remote(low, low, {"x": xp}), remote(high, high, {"x": xm})]

    def s8(c):
        for copy in done["cgx2", c]:
            copy.wait_recv()
        src = iq.at[k, c, pl.ds(al((1 - k) * cols, cols), cols)]
        done["iq", c] = remote(src, src, {"k": 1 - k})

    def s9(c):
        done["ir", c].wait_recv()
        done["iq", c].wait_recv()

        @pl.loop(0, steps)
        def _(i):
            m = pl.ds(al(i * block, block), block)
            acc = cb[m, :]
            for p in range(2):
                acc += lax.dot_general(
                    ir[p, c, m, :], iq[p, c, pl.ds(al(k * cols, cols), cols), :],
                    (((1,), (1,)), ((), ())), preferred_element_type=F32,
                )
            cb[m, :] = acc

    c_own.wait()
    stages = [s1, s2, s3, s4, s5, s6, s7, s8, s9]
    order = sorted(
        (turn * SPREAD + n, n, CHUNKS - 1 - turn) for turn in range(CHUNKS) for n in range(len(stages))
    )
    for _, n, c in order:
        stages[n](c)
    result = here(cb, out_ref)
    for copy in sent:
        copy.wait_send()
    for c in range(CHUNKS):
        @pl.when(jnp.logical_not(diagonal))
        def _():
            done["tr", c][0].wait_send()
    result.wait()


def solution(mesh):
    devices = mesh.devices
    split = Mesh(devices.reshape(2, 4, 2, 4, 2), AXES)

    def body(held, factor, inverses, covariance):
        rows, cols = held.shape
        fcols = factor.shape[2]
        drows, width = inverses.shape[1:]
        wide = width // CHUNKS
        part = rows // 8
        n_remote = 19 + 2 + 1 + 2 + 2 + 2 + 19 * CHUNKS
        return pl.pallas_call(
            kernel,
            out_shape=jax.ShapeDtypeStruct(covariance.shape, covariance.dtype),
            in_specs=[pl.BlockSpec(memory_space=pl.ANY)] * 4,
            out_specs=pl.BlockSpec(memory_space=pl.ANY),
            scratch_shapes=[
                pltpu.VMEM((2, rows, cols), BF16),
                pltpu.VMEM((4, 2 * cols, 2 * fcols), BF16),
                pltpu.VMEM((8, 8, drows // 8, width), BF16),
                pltpu.VMEM((2 * cols, wide), BF16),
                pltpu.VMEM((CHUNKS, rows, wide), BF16),
                pltpu.VMEM((CHUNKS, part, wide), F32),
                pltpu.VMEM((CHUNKS, 2, part, wide), BF16),
                pltpu.VMEM((CHUNKS, 2, 2 * part, wide), BF16),
                pltpu.VMEM((CHUNKS, 2, part, wide), BF16),
                pltpu.VMEM((2, CHUNKS, rows, wide), BF16),
                pltpu.VMEM((2, CHUNKS, rows, wide), BF16),
                pltpu.VMEM((rows, cols), F32),
                pltpu.SemaphoreType.DMA((n_remote,)),
                pltpu.SemaphoreType.DMA((n_remote,)),
                pltpu.SemaphoreType.DMA((8,)),
            ],
            compiler_params=pltpu.CompilerParams(
                collective_id=0, has_side_effects=True, vmem_limit_bytes=60 * 1024 * 1024
            ),
        )(held, factor, inverses, covariance)

    spec = P(("x", "zh"), ("zl", "y", "k"))
    return jax.shard_map(
        body,
        mesh=split,
        in_specs=(spec, P(None, ("zl", "y", "k"), ("x", "zh")), P(None, ("x", "zh"), None), spec),
        out_specs=spec,
        check_vma=False,
    )
```

```python
import jax
import jax.numpy as jnp
from jax import lax
from jax.experimental import pallas as pl
from jax.experimental.pallas import tpu as pltpu
from jax.sharding import Mesh
from jax.sharding import PartitionSpec as P

MESH = pl.DeviceIdType.MESH
AXES = ("zl", "x", "zh", "y", "k")
BF16 = jnp.bfloat16
F32 = jnp.float32

CHUNKS = 4
SUB = 2
START, PERIOD = 20.0, 2.7
TIMES = (0.0, 2.8, 5.6, 8.4, 11.2, 13.9, 16.6, 19.3, 22.0)


def al(i, n):
    return pl.multiple_of(i, n)


def kernel(
    l_ref, f_ref, d_ref, c_ref, out_ref,
    lb, g, db, s, t, own, rs1, rs2, rsz, ir, iq, cb, send, recv, send_f, recv_f, send_a, local,
):
    zl, x, zh, y, k = (lax.axis_index(a) for a in AXES)
    rows, cols = l_ref.shape
    _, _, fcols = f_ref.shape
    drows, width = d_ref.shape[1:]
    wide = width // CHUNKS
    part = rows // 8
    pair = 2 * part
    r = 2 * x + zh
    xp, xm = lax.rem(x + 1, 4), lax.rem(x + 3, 4)
    yp, ym, y2 = lax.rem(y + 1, 4), lax.rem(y + 3, 4), lax.rem(y + 2, 4)
    piece = 2 * y + zl

    ys, zs = 2 * lax.rem(x, 2) + zh, x // 2
    d_to, e_to = lax.rem(y - ys + 4, 4), lax.rem(zl + zs, 2)
    tr_to = {"zl": zs, "x": lax.rem(x + d_to, 4), "zh": lax.rem(zh + e_to, 2), "y": ys}
    xs, hs = 2 * zl + y // 2, lax.rem(y, 2)
    d_from, e_from = lax.rem(x - xs + 4, 4), lax.rem(zh + hs, 2)
    tr_from = {"zl": lax.rem(zl + e_from, 2), "x": xs, "zh": hs, "y": lax.rem(y + d_from, 4)}
    diagonal = jnp.logical_and(d_to == 0, e_to == 0)
    got = 2 * lax.rem(y + d_from, 4) + lax.rem(zl + e_from, 2)
    gotz = 2 * lax.rem(y + d_from, 4) + lax.rem(zl + e_from + 1, 2)
    bx = lax.rem(y + d_from, 4)
    bxp, bxm = lax.rem(bx + 1, 4), lax.rem(bx + 3, 4)

    group = [
        {"x": lax.rem(x + dx, 4), "zh": lax.rem(zh + dz, 2)}
        for dx in range(4) for dz in range(2) if dx or dz
    ]
    peers = group + [
        {"k": 1 - k}, {"zh": 1 - zh, "k": 1 - k}, {"x": xp, "k": 1 - k}, {"x": xm, "k": 1 - k},
        {"zl": 1 - zl}, {"y": yp}, {"y": ym},
    ]
    barrier = pltpu.get_barrier_semaphore()
    for peer in peers:
        pl.semaphore_signal(barrier, inc=1, device_id=peer, device_id_type=MESH)

    @pl.when(jnp.logical_not(diagonal))
    def _():
        pl.semaphore_signal(barrier, inc=1, device_id=tr_to, device_id_type=MESH)
        pl.semaphore_signal(barrier, inc=1, device_id=tr_from, device_id_type=MESH)
        pl.semaphore_wait(barrier, len(peers) + 2)

    @pl.when(diagonal)
    def _():
        pl.semaphore_wait(barrier, len(peers))

    counts = {"remote": 0, "local": 0}
    sent = []

    def remote(src, dst, device):
        n = counts["remote"]
        counts["remote"] += 1
        copy = pltpu.make_async_remote_copy(
            src_ref=src, dst_ref=dst, send_sem=send.at[n], recv_sem=recv.at[n],
            device_id=device, device_id_type=MESH,
        )
        sent.append(copy)
        copy.start()
        return copy

    def here(src, dst):
        n = counts["local"]
        counts["local"] += 1
        copy = pltpu.make_async_copy(src, dst, local.at[n])
        copy.start()
        return copy

    dpart = drows // 8
    dsrc = d_ref.at[k, pl.ds(al(piece * dpart, dpart), dpart), :]
    d_own = here(dsrc, db.at[r, piece])
    d_r = [remote(dsrc, db.at[r, piece], peer) for peer in group]

    sub = cols // SUB

    def rows_f(h, u):
        return pl.ds(al(h * cols + u * sub, sub), sub)

    def lanes_f(hh):
        return pl.ds(al(hh * fcols, fcols), fcols)

    def src_f(p, u):
        return f_ref.at[p, pl.ds(u * sub, sub), :]

    slots = [g.at[x, rows_f(k, u), lanes_f(zh)] for u in range(SUB)]
    f_z = [
        [
            remote(src_f(k, u), slots[u], {"zh": 1 - zh}),
            remote(src_f(1 - k, u), slots[u], {"zh": 1 - zh, "k": 1 - k}),
        ]
        for u in range(SUB)
    ]

    def hop(c, h, ab, u):
        n = ((c * 2 + h) * 2 + ab) * SUB + u
        ref = g.at[c, rows_f(h, u), lanes_f(1 - zh if ab else zh)]
        return pltpu.make_async_remote_copy(
            src_ref=ref, dst_ref=ref, send_sem=send_f.at[n], recv_sem=recv_f.at[n],
            device_id={"x": xm if h else xp}, device_id_type=MESH,
        )

    ahead = jnp.where(k == 0, xp, xm)
    f_a = []
    for u in range(SUB):
        n = (x * 2 + k) * 2 * SUB + u
        for p, device in ((k, {"x": ahead}), (1 - k, {"x": ahead, "k": 1 - k})):
            copy = pltpu.make_async_remote_copy(
                src_ref=src_f(p, u), dst_ref=slots[u], send_sem=send_a.at[len(f_a)], recv_sem=recv_f.at[n],
                device_id=device, device_id_type=MESH,
            )
            copy.start()
            f_a.append(copy)
    own_slot = g.at[x, pl.ds(al(k * cols, cols), cols), lanes_f(zh)]
    f_own = here(f_ref.at[k], own_slot)
    f_k = remote(f_ref.at[1 - k], own_slot, {"k": 1 - k})
    l_own = here(l_ref, lb.at[k])
    l_k = remote(l_ref, lb.at[k], {"k": 1 - k})
    c_own = here(c_ref, cb)
    done = {}
    moved = []

    def when_at(c, n):
        return lax.rem(x - c + 4, 4) == n

    def relay(c, ab, u, n):
        for h in range(2):
            if n == 0 and ab == 0:
                continue
            @pl.when(when_at(c, (4 - n) % 4 if h else n))
            def _():
                copy = hop(c, h, ab, u)
                if n > 0:
                    copy.wait_recv()
                if n < 3:
                    copy.start()
            if n < 3:
                moved.append((c, h, ab, u, n))

    def zwait(u):
        for copy in f_z[u]:
            copy.wait_recv()

    def dview(c, q):
        return db.at[pl.ds(2 * c, 8 - 2 * c), q, :, pl.ds(c * wide, wide)]

    def d1(c):
        if c == CHUNKS - 1:
            d_own.wait()
            for copy in d_r:
                copy.wait_recv()
        src = dview(c, piece)
        done["dz", c] = remote(src, src, {"zl": 1 - zl})

    def d2(c):
        done["dz", c].wait_recv()
        src = dview(c, pl.ds(2 * y, 2))
        done["dy", c] = [remote(src, src, {"y": yp}), remote(src, src, {"y": ym})]

    def d3(c):
        for copy in done["dy", c]:
            copy.wait_recv()
        low, high = dview(c, 2 * ym), dview(c, 2 * yp + 1)
        done["dy2", c] = [remote(low, low, {"y": yp}), remote(high, high, {"y": ym})]

    def d4(c):
        for copy in done["dy2", c]:
            copy.wait_recv()

    def base():
        f_own.wait()
        f_k.wait_recv()
        l_own.wait()
        l_k.wait_recv()

    block = 512
    steps = rows // block

    def slab(b):
        return pl.ds(al(b * pair, pair), pair)

    def thin(p):
        return pl.ds(al(p * part, part), part)

    def s1(c):
        lanes = slice(c * wide, (c + 1) * wide)
        first = c * wide // (2 * drows)

        @pl.loop(0, steps)
        def _(i):
            m = pl.ds(al(i * block, block), block)
            acc = None
            for xx in range(first, 4):
                rhs = db[2 * xx : 2 * xx + 2, :, :, lanes].reshape(2 * drows, wide)
                term = jnp.dot(g[xx, m, :], rhs, preferred_element_type=F32)
                acc = term if acc is None else acc + term
            s[m, :] = acc.astype(BF16)

        @pl.loop(0, steps)
        def _(i):
            m = pl.ds(al(i * block, block), block)
            acc = jnp.dot(lb[0, m, :], s[:cols, :], preferred_element_type=F32)
            acc += jnp.dot(lb[1, m, :], s[cols:, :], preferred_element_type=F32)
            t[c, m, :] = acc.astype(BF16)

        done["rs1", c] = [
            remote(t.at[c, thin(2 * y2)], rs1.at[c, 0], {"y": yp}),
            remote(t.at[c, thin(2 * y2 + 1)], rs1.at[c, 1], {"y": ym}),
        ]

    def s2(c):
        up, down = done["rs1", c]
        up.wait_recv()
        t[c, thin(2 * yp), :] = (t[c, thin(2 * yp), :].astype(F32) + rs1[c, 0].astype(F32)).astype(BF16)
        down.wait_recv()
        t[c, thin(2 * ym + 1), :] = (t[c, thin(2 * ym + 1), :].astype(F32) + rs1[c, 1].astype(F32)).astype(BF16)
        done["rs2", c] = [
            remote(t.at[c, slab(yp)], rs2.at[c, 0], {"y": yp}),
            remote(t.at[c, slab(ym)], rs2.at[c, 1], {"y": ym}),
        ]

    def s3(c):
        for copy in done["rs2", c]:
            copy.wait_recv()
        away = 1 - zl
        for dst, z in ((rsz.at[c, 0], away), (own.at[c], zl)):
            total = t[c, thin(2 * y + z), :].astype(F32)
            for side in range(2):
                total += rs2[c, side, pl.ds(al(z * part, part), part), :].astype(F32)
            dst[...] = total.astype(dst.dtype)
        done["rsz", c] = remote(rsz.at[c, 0], rsz.at[c, 1], {"zl": 1 - zl})

    def s4(c):
        done["rsz", c].wait_recv()
        ir[k, c, thin(piece), :] = (-(own[c] + rsz[c, 1].astype(F32))).astype(BF16)
        src = ir.at[k, c, thin(piece)]
        done["agz", c] = remote(src, src, {"zl": 1 - zl})
        n = counts["remote"]
        counts["remote"] += 1
        dst = iq.at[k, c, thin(piece)]
        away = pltpu.make_async_remote_copy(
            src_ref=src, dst_ref=dst, send_sem=send.at[n], recv_sem=recv.at[n], device_id=tr_to, device_id_type=MESH
        )
        still = pltpu.make_async_copy(src, dst, recv.at[n])
        done["tr", c] = away, still

        @pl.when(jnp.logical_not(diagonal))
        def _():
            away.start()

        @pl.when(diagonal)
        def _():
            still.start()

    def s5(c):
        done["agz", c].wait_recv()
        src = ir.at[k, c, slab(y)]
        done["agy", c] = [remote(src, src, {"y": yp}), remote(src, src, {"y": ym})]
        away, still = done["tr", c]

        @pl.when(jnp.logical_not(diagonal))
        def _():
            away.wait_recv()

        @pl.when(diagonal)
        def _():
            still.wait()

        src = iq.at[k, c, thin(got)]
        done["cgz", c] = remote(src, src, {"zh": 1 - zh})

    def s6(c):
        for copy in done["agy", c]:
            copy.wait_recv()
        low, high = ir.at[k, c, thin(2 * ym)], ir.at[k, c, thin(2 * yp + 1)]
        done["agy2", c] = [remote(low, low, {"y": yp}), remote(high, high, {"y": ym})]
        done["cgz", c].wait_recv()
        src = iq.at[k, c, slab(bx)]
        done["cgx", c] = [remote(src, src, {"x": xp}), remote(src, src, {"x": xm})]

    def s7(c):
        for copy in done["agy2", c]:
            copy.wait_recv()
        done["ir", c] = remote(ir.at[k, c], ir.at[k, c], {"k": 1 - k})
        for copy in done["cgx", c]:
            copy.wait_recv()
        low, high = iq.at[k, c, thin(2 * bxm)], iq.at[k, c, thin(2 * bxp + 1)]
        done["cgx2", c] = [remote(low, low, {"x": xp}), remote(high, high, {"x": xm})]

    def s8(c):
        for copy in done["cgx2", c]:
            copy.wait_recv()
        src = iq.at[k, c, pl.ds(al((1 - k) * cols, cols), cols)]
        done["iq", c] = remote(src, src, {"k": 1 - k})

    def s9(c):
        done["ir", c].wait_recv()
        done["iq", c].wait_recv()

        @pl.loop(0, steps)
        def _(i):
            m = pl.ds(al(i * block, block), block)
            acc = cb[m, :]
            for p in range(2):
                acc += lax.dot_general(
                    ir[p, c, m, :], iq[p, c, pl.ds(al(k * cols, cols), cols), :],
                    (((1,), (1,)), ((), ())), preferred_element_type=F32,
                )
            cb[m, :] = acc

    stages = [s1, s2, s3, s4, s5, s6, s7, s8, s9]
    plan = [(START - 0.1, base, ()), (START + TIMES[8] - 0.1, c_own.wait, ())]
    for u in range(SUB):
        plan.append((8.0 + 2.0 * u, zwait, (u,)))
    for turn in range(CHUNKS):
        c = CHUNKS - 1 - turn
        for n, step in enumerate((d1, d2, d3, d4)):
            plan.append((5.5 + 3.5 * n + 2.0 * turn, step, (c,)))
        for u in range(SUB):
            for ab in range(2):
                for n in range(4):
                    when = (8.0 + 0.1 if ab else 2.0) + 2.0 * u + 4.0 * n + 2.0 * turn
                    plan.append((when, relay, (c, ab, u, n)))
        last = max(when for when, step, args in plan if step in (relay, d4) and args[0] == c)
        begin = max(START + PERIOD * turn, last + 0.01)
        for n, step in enumerate(stages):
            plan.append((begin + TIMES[n], step, (c,)))
    for when, step, args in sorted(plan, key=lambda item: item[0]):
        step(*args)
    result = here(cb, out_ref)
    for copy in sent + f_a:
        copy.wait_send()
    for c, h, ab, u, n in moved:
        @pl.when(when_at(c, (4 - n) % 4 if h else n))
        def _():
            hop(c, h, ab, u).wait_send()
    for c in range(CHUNKS):
        @pl.when(jnp.logical_not(diagonal))
        def _():
            done["tr", c][0].wait_send()
    result.wait()


def solution(mesh):
    devices = mesh.devices
    split = Mesh(devices.reshape(2, 4, 2, 4, 2), AXES)

    def body(held, factor, inverses, covariance):
        rows, cols = held.shape
        fcols = factor.shape[2]
        drows, width = inverses.shape[1:]
        wide = width // CHUNKS
        part = rows // 8
        n_remote = 9 + 2 * SUB + 23 * CHUNKS
        return pl.pallas_call(
            kernel,
            out_shape=jax.ShapeDtypeStruct(covariance.shape, covariance.dtype),
            in_specs=[pl.BlockSpec(memory_space=pl.ANY)] * 4,
            out_specs=pl.BlockSpec(memory_space=pl.ANY),
            scratch_shapes=[
                pltpu.VMEM((2, rows, cols), BF16),
                pltpu.VMEM((4, 2 * cols, 2 * fcols), BF16),
                pltpu.VMEM((8, 8, drows // 8, width), BF16),
                pltpu.VMEM((2 * cols, wide), BF16),
                pltpu.VMEM((CHUNKS, rows, wide), BF16),
                pltpu.VMEM((CHUNKS, part, wide), F32),
                pltpu.VMEM((CHUNKS, 2, part, wide), BF16),
                pltpu.VMEM((CHUNKS, 2, 2 * part, wide), BF16),
                pltpu.VMEM((CHUNKS, 2, part, wide), BF16),
                pltpu.VMEM((2, CHUNKS, rows, wide), BF16),
                pltpu.VMEM((2, CHUNKS, rows, wide), BF16),
                pltpu.VMEM((rows, cols), F32),
                pltpu.SemaphoreType.DMA((n_remote,)),
                pltpu.SemaphoreType.DMA((n_remote,)),
                pltpu.SemaphoreType.DMA((16 * SUB,)),
                pltpu.SemaphoreType.DMA((16 * SUB,)),
                pltpu.SemaphoreType.DMA((2 * SUB,)),
                pltpu.SemaphoreType.DMA((8,)),
            ],
            compiler_params=pltpu.CompilerParams(
                collective_id=0, has_side_effects=True, vmem_limit_bytes=60 * 1024 * 1024
            ),
        )(held, factor, inverses, covariance)

    spec = P(("x", "zh"), ("zl", "y", "k"))
    return jax.shard_map(
        body,
        mesh=split,
        in_specs=(spec, P(None, ("zl", "y", "k"), ("x", "zh")), P(None, ("x", "zh"), None), spec),
        out_specs=spec,
        check_vma=False,
    )
```

```python
import jax
import jax.numpy as jnp
from jax import lax
from jax.experimental import pallas as pl
from jax.experimental.pallas import tpu as pltpu
from jax.sharding import Mesh
from jax.sharding import PartitionSpec as P

MESH = pl.DeviceIdType.MESH
AXES = ("zl", "x", "zh", "y", "k")
BF16 = jnp.bfloat16
F32 = jnp.float32

CHUNKS = 4
SUB = 2
ORDER = (
    (1,0), (0,0,0,1,1), (0,1,0,0,1), (0,2,0,0,1), (0,1,0,1,1), (0,3,0,0,1), (0,0,0,0,1), (0,2,0,1,1), (0,2,1,0,0),
    (1,1), (0,1,1,0,0), (0,3,0,1,1), (0,0,1,0,0), (0,3,1,1,0), (0,3,0,0,2), (0,2,0,0,2), (0,2,1,1,0), (0,1,0,0,2),
    (0,3,1,0,0), (0,0,0,0,2), (0,2,0,1,2), (0,1,1,0,1), (0,2,1,1,1), (0,0,1,1,0), (0,0,0,1,2), (0,1,1,1,0),
    (0,1,0,1,2), (0,3,1,0,1), (0,0,1,0,1), (3,1), (3,2), (0,3,0,1,2), (3,0), (3,3), (0,2,1,0,1), (0,2,0,0,3),
    (0,1,1,1,1), (0,3,1,1,1), (4,1), (0,0,1,1,1), (0,1,1,1,2), (0,2,1,1,2), (0,0,0,0,3), (0,3,0,0,3), (4,2),
    (0,2,1,0,2), (0,0,1,0,2), (0,1,1,0,2), (0,3,1,0,2), (0,3,1,1,2), (4,0), (4,3), (0,0,1,1,2), (0,1,1,1,3),
    (0,3,1,0,3), (0,1,0,0,3), (0,0,1,0,3), (0,2,1,1,3), (0,3,1,1,3), (5,1), (0,2,0,1,3), (0,3,0,1,3), (0,1,1,0,3),
    (0,1,0,1,3), (0,2,1,0,3), (0,0,0,1,3), (5,2), (6,2), (6,1), (5,3), (0,0,1,1,3), (7,2), (5,0), (7,1), (6,0),
    (8,2), (6,3), (8,1), (7,0), (9,2), (9,1), (11,2), (7,3), (8,0), (11,1), (10,1), (13,2), (10,2), (8,3), (9,0),
    (13,1), (9,3), (10,3), (15,2), (11,0), (12,1), (15,1), (11,3), (10,0), (13,0), (13,3), (12,0), (16,2), (15,0),
    (16,1), (12,2), (14,1), (15,3), (14,0), (17,1), (14,2), (12,3), (16,0), (16,3), (17,2), (14,3), (17,0), (17,3),
)


def al(i, n):
    return pl.multiple_of(i, n)


def kernel(
    l_ref, f_ref, d_ref, c_ref, cb, irl_ref, iql_ref,
    lb, g, db, s, t, own, rs1, rs2, rsz, ir, iq, send, recv, send_f, recv_f, send_a, send_d, recv_d, local_d, send_x, recv_x, local,
):
    zl, x, zh, y, k = (lax.axis_index(a) for a in AXES)
    rows, cols = l_ref.shape
    _, _, fcols = f_ref.shape
    drows, width = d_ref.shape[1:]
    wide = width // CHUNKS
    part = rows // 8
    pair = 2 * part
    r = 2 * x + zh
    xp, xm = lax.rem(x + 1, 4), lax.rem(x + 3, 4)
    yp, ym, y2 = lax.rem(y + 1, 4), lax.rem(y + 3, 4), lax.rem(y + 2, 4)
    piece = 2 * y + zl

    ys, zs = 2 * lax.rem(x, 2) + zh, x // 2
    d_to, e_to = lax.rem(y - ys + 4, 4), lax.rem(zl + zs, 2)
    tr_to = {"zl": zs, "x": lax.rem(x + d_to, 4), "zh": lax.rem(zh + e_to, 2), "y": ys}
    xs, hs = 2 * zl + y // 2, lax.rem(y, 2)
    d_from, e_from = lax.rem(x - xs + 4, 4), lax.rem(zh + hs, 2)
    tr_from = {"zl": lax.rem(zl + e_from, 2), "x": xs, "zh": hs, "y": lax.rem(y + d_from, 4)}
    diagonal = jnp.logical_and(d_to == 0, e_to == 0)
    got = 2 * lax.rem(y + d_from, 4) + lax.rem(zl + e_from, 2)
    gotz = 2 * lax.rem(y + d_from, 4) + lax.rem(zl + e_from + 1, 2)
    bx = lax.rem(y + d_from, 4)
    bxp, bxm = lax.rem(bx + 1, 4), lax.rem(bx + 3, 4)

    shifts = [(dx, dz) for dx in range(4) for dz in range(2) if dx or dz]
    group = [
        {"x": lax.rem(x + dx, 4), "zh": lax.rem(zh + dz, 2), "zl": lax.rem(zl + dz, 2)} for dx, dz in shifts
    ]
    peers = group + [
        {"zh": 1 - zh},
        {"k": 1 - k}, {"zh": 1 - zh, "k": 1 - k}, {"x": xp, "k": 1 - k}, {"x": xm, "k": 1 - k},
        {"zl": 1 - zl}, {"y": yp}, {"y": ym},
    ]
    barrier = pltpu.get_barrier_semaphore()
    for peer in peers:
        pl.semaphore_signal(barrier, inc=1, device_id=peer, device_id_type=MESH)

    @pl.when(jnp.logical_not(diagonal))
    def _():
        pl.semaphore_signal(barrier, inc=1, device_id=tr_to, device_id_type=MESH)
        pl.semaphore_signal(barrier, inc=1, device_id=tr_from, device_id_type=MESH)
        pl.semaphore_wait(barrier, len(peers) + 2)

    @pl.when(diagonal)
    def _():
        pl.semaphore_wait(barrier, len(peers))

    final = [entry for entry in ORDER if entry[0] == 17][-1][1]
    irs = {c: ir.at[:, n] for n, c in enumerate(c for c in range(CHUNKS) if c != final)}
    iqs = {c: iq.at[:, n] for n, c in enumerate(c for c in range(CHUNKS) if c != final)}
    irs[final], iqs[final] = irl_ref, iql_ref
    counts = {"remote": 0, "local": 0}
    sent = []

    def remote(src, dst, device):
        n = counts["remote"]
        counts["remote"] += 1
        copy = pltpu.make_async_remote_copy(
            src_ref=src, dst_ref=dst, send_sem=send.at[n], recv_sem=recv.at[n],
            device_id=device, device_id_type=MESH,
        )
        sent.append(copy)
        copy.start()
        return copy

    def here(src, dst):
        n = counts["local"]
        counts["local"] += 1
        copy = pltpu.make_async_copy(src, dst, local.at[n])
        copy.start()
        return copy

    dpart = drows // 4

    def d_copy(c, n):
        lanes = pl.ds(c * wide, wide)
        src = d_ref.at[k, pl.ds(al(y * dpart, dpart), dpart), lanes]
        dst = db.at[r, y, :, lanes]
        if n < 0:
            return pltpu.make_async_copy(src, dst, local_d.at[c])
        return pltpu.make_async_remote_copy(
            src_ref=src, dst_ref=dst, send_sem=send_d.at[c, n], recv_sem=recv_d.at[c, n],
            device_id=group[n], device_id_type=MESH,
        )

    def d_spread(c):
        @pl.when(x >= c)
        def _():
            for n in range(-1, len(group)):
                d_copy(c, n).start()

    d_spread(CHUNKS - 1)

    sub = cols // SUB

    def rows_f(h, u):
        return pl.ds(al(h * cols + u * sub, sub), sub)

    def lanes_f(hh):
        return pl.ds(al(hh * fcols, fcols), fcols)

    def src_f(p, u):
        return f_ref.at[p, pl.ds(u * sub, sub), :]

    slots = [g.at[x, rows_f(k, u), lanes_f(zh)] for u in range(SUB)]
    f_z = [
        [
            remote(src_f(k, u), slots[u], {"zh": 1 - zh}),
            remote(src_f(1 - k, u), slots[u], {"zh": 1 - zh, "k": 1 - k}),
        ]
        for u in range(SUB)
    ]

    def hop(c, h, ab, u):
        n = ((c * 2 + h) * 2 + ab) * SUB + u
        ref = g.at[c, rows_f(h, u), lanes_f(1 - zh if ab else zh)]
        return pltpu.make_async_remote_copy(
            src_ref=ref, dst_ref=ref, send_sem=send_f.at[n], recv_sem=recv_f.at[n],
            device_id={"x": xm if h else xp}, device_id_type=MESH,
        )

    ahead = jnp.where(k == 0, xp, xm)
    f_a = []
    for u in range(SUB):
        n = (x * 2 + k) * 2 * SUB + u
        for p, device in ((k, {"x": ahead}), (1 - k, {"x": ahead, "k": 1 - k})):
            copy = pltpu.make_async_remote_copy(
                src_ref=src_f(p, u), dst_ref=slots[u], send_sem=send_a.at[len(f_a)], recv_sem=recv_f.at[n],
                device_id=device, device_id_type=MESH,
            )
            copy.start()
            f_a.append(copy)
    own_slot = g.at[x, pl.ds(al(k * cols, cols), cols), lanes_f(zh)]
    f_own = here(f_ref.at[k], own_slot)
    f_k = remote(f_ref.at[1 - k], own_slot, {"k": 1 - k})
    l_own = here(l_ref, lb.at[k])
    l_k = remote(l_ref, lb.at[k], {"k": 1 - k})
    c_own = here(c_ref, cb)
    done = {}

    def when_at(c, n):
        return lax.rem(x - c + 4, 4) == n

    def across(c, h, u):
        n = (c * 2 + h) * SUB + u
        ref = g.at[c, rows_f(h, u), lanes_f(zh)]
        return pltpu.make_async_remote_copy(
            src_ref=ref, dst_ref=ref, send_sem=send_x.at[n], recv_sem=recv_x.at[n],
            device_id={"zh": 1 - zh}, device_id_type=MESH,
        )

    def relay(c, ab, u, n):
        if ab == 0:
            for h in range(2):
                @pl.when(when_at(c, (4 - n) % 4 if h else n))
                def _():
                    copy = hop(c, h, 0, u)
                    copy.wait_recv()
                    if n < 3:
                        copy.start()
            return

        at = when_at(c, 0) if n == 0 else when_at(c, 2)
        if n == 3:
            at = jnp.logical_or(when_at(c, 1), when_at(c, 3))

        @pl.when(at)
        def _():
            for h in range(2):
                if n == 1:
                    across(c, h, u).start()
                    continue
                if n == 2:
                    across(c, h, u).wait_recv()
                if n == 3:
                    hop(c, h, 1, u).wait_recv()
                else:
                    hop(c, h, 1, u).start()

    def zwait(u):
        for copy in f_z[u]:
            copy.wait_recv()

    for c in range(CHUNKS - 2, -1, -1):
        d_spread(c)

    def dview(c, q, rows_d):
        return db.at[pl.ds(2 * c, 8 - 2 * c), q, rows_d, pl.ds(c * wide, wide)]

    def d1(c):
        pass

    def d2(c):
        @pl.when(x >= c)
        def _():
            d_copy(c, -1).wait()

        for n, (dx, _) in enumerate(shifts):
            @pl.when(lax.rem(x - dx + 4, 4) >= c)
            def _():
                d_copy(c, n).wait_recv()
        src = dview(c, y, pl.ds(0, dpart))
        done["dy", c] = [remote(src, src, {"y": yp}), remote(src, src, {"y": ym})]

    def d3(c):
        for copy in done["dy", c]:
            copy.wait_recv()
        half = dpart // 2
        low, high = dview(c, ym, pl.ds(0, half)), dview(c, yp, pl.ds(half, half))
        done["dy2", c] = [remote(low, low, {"y": yp}), remote(high, high, {"y": ym})]

    def d4(c):
        for copy in done["dy2", c]:
            copy.wait_recv()

    def base():
        f_own.wait()
        f_k.wait_recv()
        l_own.wait()
        l_k.wait_recv()

    block = 512
    steps = rows // block

    def slab(b):
        return pl.ds(al(b * pair, pair), pair)

    def thin(p):
        return pl.ds(al(p * part, part), part)

    def s1(c):
        lanes = slice(c * wide, (c + 1) * wide)
        first = c * wide // (2 * drows)

        @pl.loop(0, steps)
        def _(i):
            m = pl.ds(al(i * block, block), block)
            acc = None
            for xx in range(first, 4):
                rhs = db[2 * xx : 2 * xx + 2, :, :, lanes].reshape(2 * drows, wide)
                term = jnp.dot(g[xx, m, :], rhs, preferred_element_type=F32)
                acc = term if acc is None else acc + term
            s[m, :] = acc.astype(BF16)

        @pl.loop(0, steps)
        def _(i):
            m = pl.ds(al(i * block, block), block)
            acc = jnp.dot(lb[0, m, :], s[:cols, :], preferred_element_type=F32)
            acc += jnp.dot(lb[1, m, :], s[cols:, :], preferred_element_type=F32)
            t[c, m, :] = acc.astype(BF16)

        done["rs1", c] = [
            remote(t.at[c, thin(2 * y2)], rs1.at[c, 0], {"y": yp}),
            remote(t.at[c, thin(2 * y2 + 1)], rs1.at[c, 1], {"y": ym}),
        ]

    def s2(c):
        up, down = done["rs1", c]
        up.wait_recv()
        t[c, thin(2 * yp), :] = (t[c, thin(2 * yp), :].astype(F32) + rs1[c, 0].astype(F32)).astype(BF16)
        down.wait_recv()
        t[c, thin(2 * ym + 1), :] = (t[c, thin(2 * ym + 1), :].astype(F32) + rs1[c, 1].astype(F32)).astype(BF16)
        done["rs2", c] = [
            remote(t.at[c, slab(yp)], rs2.at[c, 0], {"y": yp}),
            remote(t.at[c, slab(ym)], rs2.at[c, 1], {"y": ym}),
        ]

    def s3(c):
        for copy in done["rs2", c]:
            copy.wait_recv()
        away = 1 - zl
        for dst, z in ((rsz.at[c, 0], away), (own.at[c], zl)):
            total = t[c, thin(2 * y + z), :].astype(F32)
            for side in range(2):
                total += rs2[c, side, pl.ds(al(z * part, part), part), :].astype(F32)
            dst[...] = total.astype(dst.dtype)
        done["rsz", c] = remote(rsz.at[c, 0], rsz.at[c, 1], {"zl": 1 - zl})

    def s4(c):
        done["rsz", c].wait_recv()
        irs[c][k, thin(piece), :] = (-(own[c] + rsz[c, 1].astype(F32))).astype(BF16)
        src = irs[c].at[k, thin(piece)]
        done["agz", c] = remote(src, src, {"zl": 1 - zl})
        n = counts["remote"]
        counts["remote"] += 1
        dst = iqs[c].at[k, thin(piece)]
        away = pltpu.make_async_remote_copy(
            src_ref=src, dst_ref=dst, send_sem=send.at[n], recv_sem=recv.at[n], device_id=tr_to, device_id_type=MESH
        )
        still = pltpu.make_async_copy(src, dst, recv.at[n])
        done["tr", c] = away, still

        @pl.when(jnp.logical_not(diagonal))
        def _():
            away.start()

        @pl.when(diagonal)
        def _():
            still.start()

    def s5a(c):
        done["agz", c].wait_recv()
        src = irs[c].at[k, slab(y)]
        done["agy", c] = [remote(src, src, {"y": yp}), remote(src, src, {"y": ym})]

    def s5b(c):
        away, still = done["tr", c]

        @pl.when(jnp.logical_not(diagonal))
        def _():
            away.wait_recv()

        @pl.when(diagonal)
        def _():
            still.wait()

        src = iqs[c].at[k, thin(got)]
        done["cgz", c] = remote(src, src, {"zh": 1 - zh})

    def s6a(c):
        for copy in done["agy", c]:
            copy.wait_recv()
        low, high = irs[c].at[k, thin(2 * ym)], irs[c].at[k, thin(2 * yp + 1)]
        done["agy2", c] = [remote(low, low, {"y": yp}), remote(high, high, {"y": ym})]

    def s6b(c):
        done["cgz", c].wait_recv()
        src = iqs[c].at[k, slab(bx)]
        done["cgx", c] = [remote(src, src, {"x": xp}), remote(src, src, {"x": xm})]

    def s7a(c):
        for copy in done["agy2", c]:
            copy.wait_recv()
        done["ir", c] = remote(irs[c].at[k], irs[c].at[k], {"k": 1 - k})

    def s7b(c):
        for copy in done["cgx", c]:
            copy.wait_recv()
        low, high = iqs[c].at[k, thin(2 * bxm)], iqs[c].at[k, thin(2 * bxp + 1)]
        done["cgx2", c] = [remote(low, low, {"x": xp}), remote(high, high, {"x": xm})]

    def s8(c):
        for copy in done["cgx2", c]:
            copy.wait_recv()
        src = iqs[c].at[k, pl.ds(al((1 - k) * cols, cols), cols)]
        done["iq", c] = remote(src, src, {"k": 1 - k})

    def s9(c):
        done["ir", c].wait_recv()
        done["iq", c].wait_recv()

        @pl.loop(0, steps)
        def _(i):
            m = pl.ds(al(i * block, block), block)
            acc = cb[m, :]
            for p in range(2):
                acc += lax.dot_general(
                    irs[c][p, m, :], iqs[c][p, pl.ds(al(k * cols, cols), cols), :],
                    (((1,), (1,)), ((), ())), preferred_element_type=F32,
                )
            cb[m, :] = acc

    steps_of = (relay, zwait, d1, d2, d3, d4, s1, s2, s3, s4, s5a, s5b, s6a, s6b, s7a, s7b, s8, s9)
    based = False
    added = []
    for entry in ORDER:
        step, args = steps_of[entry[0]], entry[1:]
        if step is s1 and not based:
            base()
            based = True
        if step is s9 and not added:
            c_own.wait()
        if step is s9:
            added.append(args[0])
            if len(added) == CHUNKS:
                break
        step(*args)
    done["ir", final].wait_recv()
    done["iq", final].wait_recv()
    for copy in sent + f_a:
        copy.wait_send()
    for c in range(CHUNKS):
        @pl.when(x >= c)
        def _():
            for n in range(len(group)):
                d_copy(c, n).wait_send()

        for u in range(SUB):
            for n in range(1, 3):
                for h in range(2):
                    @pl.when(when_at(c, (4 - n) % 4 if h else n))
                    def _():
                        hop(c, h, 0, u).wait_send()

            @pl.when(when_at(c, 0))
            def _():
                for h in range(2):
                    hop(c, h, 1, u).wait_send()

            @pl.when(when_at(c, 2))
            def _():
                for h in range(2):
                    across(c, h, u).wait_send()
                    hop(c, h, 1, u).wait_send()

    for c in range(CHUNKS):
        @pl.when(jnp.logical_not(diagonal))
        def _():
            done["tr", c][0].wait_send()


def last(c_ref, ir_ref, iq_ref, out_ref):
    tall, cols = out_ref.shape
    block = pl.ds(al(lax.axis_index("k") * cols, cols), cols)
    m = pl.ds(al(pl.program_id(0) * tall, tall), tall)
    total = c_ref[m, :]
    for p in range(2):
        total += lax.dot_general(
            ir_ref[p, m, :], iq_ref[p, block, :], (((1,), (1,)), ((), ())), preferred_element_type=F32
        )
    out_ref[...] = total


def solution(mesh):
    devices = mesh.devices
    split = Mesh(devices.reshape(2, 4, 2, 4, 2), AXES)

    def body(held, factor, inverses, covariance):
        rows, cols = held.shape
        fcols = factor.shape[2]
        drows, width = inverses.shape[1:]
        wide = width // CHUNKS
        part = rows // 8
        n_remote = 2 + 2 * SUB + 22 * CHUNKS
        partial_sum, left, right = pl.pallas_call(
            kernel,
            out_shape=[
                pltpu.VMEM((rows, cols), F32),
                pltpu.VMEM((2, rows, wide), BF16),
                pltpu.VMEM((2, 2 * cols, wide), BF16),
            ],
            in_specs=[pl.BlockSpec(memory_space=pltpu.HBM)] * 4,
            out_specs=[pl.BlockSpec(memory_space=pltpu.VMEM)] * 3,
            scratch_shapes=[
                pltpu.VMEM((2, rows, cols), BF16),
                pltpu.VMEM((4, 2 * cols, 2 * fcols), BF16),
                pltpu.VMEM((8, 4, drows // 4, width), BF16),
                pltpu.VMEM((2 * cols, wide), BF16),
                pltpu.VMEM((CHUNKS, rows, wide), BF16),
                pltpu.VMEM((CHUNKS, part, wide), F32),
                pltpu.VMEM((CHUNKS, 2, part, wide), BF16),
                pltpu.VMEM((CHUNKS, 2, 2 * part, wide), BF16),
                pltpu.VMEM((CHUNKS, 2, part, wide), BF16),
                pltpu.VMEM((2, CHUNKS - 1, rows, wide), BF16),
                pltpu.VMEM((2, CHUNKS - 1, rows, wide), BF16),
                pltpu.SemaphoreType.DMA((n_remote,)),
                pltpu.SemaphoreType.DMA((n_remote,)),
                pltpu.SemaphoreType.DMA((16 * SUB,)),
                pltpu.SemaphoreType.DMA((16 * SUB,)),
                pltpu.SemaphoreType.DMA((2 * SUB,)),
                pltpu.SemaphoreType.DMA((CHUNKS, 7)),
                pltpu.SemaphoreType.DMA((CHUNKS, 7)),
                pltpu.SemaphoreType.DMA((CHUNKS,)),
                pltpu.SemaphoreType.DMA((8 * SUB,)),
                pltpu.SemaphoreType.DMA((8 * SUB,)),
                pltpu.SemaphoreType.DMA((8,)),
            ],
            compiler_params=pltpu.CompilerParams(
                collective_id=0, has_side_effects=True, vmem_limit_bytes=50 * 1024 * 1024
            ),
        )(held, factor, inverses, covariance)
        tall = 256
        return pl.pallas_call(
            last,
            out_shape=jax.ShapeDtypeStruct(covariance.shape, covariance.dtype),
            grid=(rows // tall,),
            in_specs=[pl.BlockSpec(memory_space=pltpu.VMEM)] * 3,
            out_specs=pl.BlockSpec((tall, cols), lambda i: (i, 0)),
            compiler_params=pltpu.CompilerParams(vmem_limit_bytes=8 * 1024 * 1024),
        )(partial_sum, left, right)

    spec = P(("x", "zh"), ("zl", "y", "k"))
    return jax.shard_map(
        body,
        mesh=split,
        in_specs=(spec, P(None, ("zl", "y", "k"), ("x", "zh")), P(None, ("x", "zh"), None), spec),
        out_specs=spec,
        check_vma=False,
    )
```

```python
import jax
import jax.numpy as jnp
from jax import lax
from jax.experimental import pallas as pl
from jax.experimental.pallas import tpu as pltpu
from jax.sharding import Mesh
from jax.sharding import PartitionSpec as P

MESH = pl.DeviceIdType.MESH
AXES = ("zl", "x", "zh", "y", "k")
BF16 = jnp.bfloat16
F32 = jnp.float32

CHUNKS = 4
SUB = 2
ORDER = (
    (0,1,0,0,1), (0,0,0,0,1), (0,0,0,1,1), (0,2,0,0,1), (1,0), (0,3,1,0,0), (0,1,1,0,0), (0,1,0,0,2), (0,3,0,0,1),
    (0,1,0,1,1), (0,2,0,1,1), (0,1,0,1,2), (1,1), (0,1,1,1,0), (0,3,0,1,1), (0,3,0,0,2), (0,3,1,0,1), (0,0,0,1,2),
    (0,2,0,0,2), (0,0,0,0,2), (0,2,1,1,0), (3,1), (0,0,1,1,0), (0,3,0,1,2), (0,2,1,0,0), (0,3,1,1,0), (0,0,1,1,1),
    (0,1,1,1,1), (3,0), (0,0,0,1,3), (0,0,1,0,0), (3,2), (0,0,1,0,1), (0,2,1,0,1), (0,1,1,0,1), (0,3,1,1,1),
    (0,2,1,0,2), (0,2,0,0,3), (3,3), (4,1), (0,3,1,0,2), (0,2,0,1,2), (0,1,1,1,2), (4,0), (0,3,1,1,2), (0,3,0,0,3),
    (0,1,0,0,3), (0,2,1,0,3), (0,2,1,1,1), (0,1,1,1,3), (0,0,1,0,2), (0,3,1,0,3), (0,0,1,1,2), (0,1,1,0,2), (4,3),
    (5,1), (0,0,0,0,3), (0,2,1,1,2), (0,1,0,1,3), (5,3), (4,2), (0,1,1,0,3), (0,3,1,1,3), (0,2,0,1,3), (0,3,0,1,3),
    (6,3), (0,0,1,0,3), (0,2,1,1,3), (5,2), (6,2), (7,3), (6,1), (5,0), (0,0,1,1,3), (7,2), (7,1), (8,3), (6,0),
    (8,2), (9,3), (9,2), (8,1), (7,0), (11,3), (9,1), (8,0), (10,2), (11,2), (13,3), (10,1), (9,0), (15,3), (11,1),
    (10,3), (10,0), (13,2), (13,1), (11,0), (12,2), (15,2), (12,3), (12,1), (16,3), (13,0), (16,2), (15,1), (14,2),
    (12,0), (14,3), (14,1), (15,0), (17,3), (16,1), (14,0), (17,2), (16,0), (17,1), (17,0),
)


def al(i, n):
    return pl.multiple_of(i, n)


def kernel(
    l_ref, f_ref, d_ref, c_ref, cb, irl_ref, iql_ref,
    lb, g, db, s, t, own, rs1, rs2, rsz, ir, iq, send, recv, send_f, recv_f, send_a, send_d, recv_d, local_d, send_x, recv_x, local,
):
    zl, x, zh, y, k = (lax.axis_index(a) for a in AXES)
    rows, cols = l_ref.shape
    _, _, fcols = f_ref.shape
    drows, width = d_ref.shape[1:]
    wide = width // CHUNKS
    part = rows // 8
    pair = 2 * part
    r = 2 * x + zh
    xp, xm = lax.rem(x + 1, 4), lax.rem(x + 3, 4)
    yp, ym, y2 = lax.rem(y + 1, 4), lax.rem(y + 3, 4), lax.rem(y + 2, 4)
    piece = 2 * y + zl

    ys, zs = 2 * lax.rem(x, 2) + zh, x // 2
    d_to, e_to = lax.rem(y - ys + 4, 4), lax.rem(zl + zs, 2)
    tr_to = {"zl": zs, "x": lax.rem(x + d_to, 4), "zh": lax.rem(zh + e_to, 2), "y": ys}
    xs, hs = 2 * zl + y // 2, lax.rem(y, 2)
    d_from, e_from = lax.rem(x - xs + 4, 4), lax.rem(zh + hs, 2)
    tr_from = {"zl": lax.rem(zl + e_from, 2), "x": xs, "zh": hs, "y": lax.rem(y + d_from, 4)}
    diagonal = jnp.logical_and(d_to == 0, e_to == 0)
    got = 2 * lax.rem(y + d_from, 4) + lax.rem(zl + e_from, 2)
    gotz = 2 * lax.rem(y + d_from, 4) + lax.rem(zl + e_from + 1, 2)
    bx = lax.rem(y + d_from, 4)
    bxp, bxm = lax.rem(bx + 1, 4), lax.rem(bx + 3, 4)

    shifts = [(dx, dz) for dx in range(4) for dz in range(2) if dx or dz]
    group = [
        {"x": lax.rem(x + dx, 4), "zh": lax.rem(zh + dz, 2), "zl": lax.rem(zl + dz, 2)} for dx, dz in shifts
    ]
    peers = group + [
        {"zh": 1 - zh},
        {"k": 1 - k}, {"zh": 1 - zh, "k": 1 - k}, {"x": xp, "k": 1 - k}, {"x": xm, "k": 1 - k},
        {"zl": 1 - zl}, {"y": yp}, {"y": ym},
    ]
    barrier = pltpu.get_barrier_semaphore()
    for peer in peers:
        pl.semaphore_signal(barrier, inc=1, device_id=peer, device_id_type=MESH)

    @pl.when(jnp.logical_not(diagonal))
    def _():
        pl.semaphore_signal(barrier, inc=1, device_id=tr_to, device_id_type=MESH)
        pl.semaphore_signal(barrier, inc=1, device_id=tr_from, device_id_type=MESH)
        pl.semaphore_wait(barrier, len(peers) + 2)

    @pl.when(diagonal)
    def _():
        pl.semaphore_wait(barrier, len(peers))

    final = [entry for entry in ORDER if entry[0] == 17][-1][1]
    irs = {c: ir.at[:, n] for n, c in enumerate(c for c in range(CHUNKS) if c != final)}
    iqs = {c: iq.at[:, n] for n, c in enumerate(c for c in range(CHUNKS) if c != final)}
    irs[final], iqs[final] = irl_ref, iql_ref
    counts = {"remote": 0, "local": 0}
    sent = []

    def remote(src, dst, device):
        n = counts["remote"]
        counts["remote"] += 1
        copy = pltpu.make_async_remote_copy(
            src_ref=src, dst_ref=dst, send_sem=send.at[n], recv_sem=recv.at[n],
            device_id=device, device_id_type=MESH,
        )
        sent.append(copy)
        copy.start()
        return copy

    def here(src, dst):
        n = counts["local"]
        counts["local"] += 1
        copy = pltpu.make_async_copy(src, dst, local.at[n])
        copy.start()
        return copy

    dpart = drows // 4

    def d_copy(c, n):
        lanes = pl.ds(c * wide, wide)
        src = d_ref.at[k, pl.ds(al(y * dpart, dpart), dpart), lanes]
        dst = db.at[r, y, :, lanes]
        if n < 0:
            return pltpu.make_async_copy(src, dst, local_d.at[c])
        return pltpu.make_async_remote_copy(
            src_ref=src, dst_ref=dst, send_sem=send_d.at[c, n], recv_sem=recv_d.at[c, n],
            device_id=group[n], device_id_type=MESH,
        )

    def d_spread(c):
        @pl.when(x >= c)
        def _():
            for n in range(-1, len(group)):
                d_copy(c, n).start()

    d_spread(CHUNKS - 1)

    sub = cols // SUB

    def rows_f(h, u):
        return pl.ds(al(h * cols + u * sub, sub), sub)

    def lanes_f(hh):
        return pl.ds(al(hh * fcols, fcols), fcols)

    def src_f(p, u):
        return f_ref.at[p, pl.ds(u * sub, sub), :]

    slots = [g.at[x, rows_f(k, u), lanes_f(zh)] for u in range(SUB)]
    f_z = [
        [
            remote(src_f(k, u), slots[u], {"zh": 1 - zh}),
            remote(src_f(1 - k, u), slots[u], {"zh": 1 - zh, "k": 1 - k}),
        ]
        for u in range(SUB)
    ]

    def hop(c, h, ab, u):
        n = ((c * 2 + h) * 2 + ab) * SUB + u
        ref = g.at[c, rows_f(h, u), lanes_f(1 - zh if ab else zh)]
        return pltpu.make_async_remote_copy(
            src_ref=ref, dst_ref=ref, send_sem=send_f.at[n], recv_sem=recv_f.at[n],
            device_id={"x": xm if h else xp}, device_id_type=MESH,
        )

    ahead = jnp.where(k == 0, xp, xm)
    f_a = []
    for u in range(SUB):
        n = (x * 2 + k) * 2 * SUB + u
        for p, device in ((k, {"x": ahead}), (1 - k, {"x": ahead, "k": 1 - k})):
            copy = pltpu.make_async_remote_copy(
                src_ref=src_f(p, u), dst_ref=slots[u], send_sem=send_a.at[len(f_a)], recv_sem=recv_f.at[n],
                device_id=device, device_id_type=MESH,
            )
            copy.start()
            f_a.append(copy)
    own_slot = g.at[x, pl.ds(al(k * cols, cols), cols), lanes_f(zh)]
    f_own = here(f_ref.at[k], own_slot)
    f_k = remote(f_ref.at[1 - k], own_slot, {"k": 1 - k})
    l_own = here(l_ref, lb.at[k])
    l_k = remote(l_ref, lb.at[k], {"k": 1 - k})
    c_own = here(c_ref, cb)
    done = {}

    def when_at(c, n):
        return lax.rem(x - c + 4, 4) == n

    def across(c, h, u):
        n = (c * 2 + h) * SUB + u
        ref = g.at[c, rows_f(h, u), lanes_f(zh)]
        return pltpu.make_async_remote_copy(
            src_ref=ref, dst_ref=ref, send_sem=send_x.at[n], recv_sem=recv_x.at[n],
            device_id={"zh": 1 - zh}, device_id_type=MESH,
        )

    def relay(c, ab, u, n):
        if ab == 0:
            for h in range(2):
                @pl.when(when_at(c, (4 - n) % 4 if h else n))
                def _():
                    copy = hop(c, h, 0, u)
                    copy.wait_recv()
                    if n < 3:
                        copy.start()
            return

        at = when_at(c, 0) if n == 0 else when_at(c, 2)
        if n == 3:
            at = jnp.logical_or(when_at(c, 1), when_at(c, 3))

        @pl.when(at)
        def _():
            for h in range(2):
                if n == 1:
                    across(c, h, u).start()
                    continue
                if n == 2:
                    across(c, h, u).wait_recv()
                if n == 3:
                    hop(c, h, 1, u).wait_recv()
                else:
                    hop(c, h, 1, u).start()

    def zwait(u):
        for copy in f_z[u]:
            copy.wait_recv()

    for c in range(CHUNKS - 2, -1, -1):
        d_spread(c)

    def dview(c, q, rows_d):
        return db.at[pl.ds(2 * c, 8 - 2 * c), q, rows_d, pl.ds(c * wide, wide)]

    def d1(c):
        pass

    def d2(c):
        @pl.when(x >= c)
        def _():
            d_copy(c, -1).wait()

        for n, (dx, _) in enumerate(shifts):
            @pl.when(lax.rem(x - dx + 4, 4) >= c)
            def _():
                d_copy(c, n).wait_recv()
        src = dview(c, y, pl.ds(0, dpart))
        done["dy", c] = [remote(src, src, {"y": yp}), remote(src, src, {"y": ym})]

    def d3(c):
        for copy in done["dy", c]:
            copy.wait_recv()
        half = dpart // 2
        low, high = dview(c, ym, pl.ds(0, half)), dview(c, yp, pl.ds(half, half))
        done["dy2", c] = [remote(low, low, {"y": yp}), remote(high, high, {"y": ym})]

    def d4(c):
        for copy in done["dy2", c]:
            copy.wait_recv()

    def base():
        f_own.wait()
        f_k.wait_recv()
        l_own.wait()
        l_k.wait_recv()

    block = 512
    steps = rows // block

    def slab(b):
        return pl.ds(al(b * pair, pair), pair)

    def thin(p):
        return pl.ds(al(p * part, part), part)

    def s1(c):
        lanes = slice(c * wide, (c + 1) * wide)
        first = c * wide // (2 * drows)

        @pl.loop(0, steps)
        def _(i):
            m = pl.ds(al(i * block, block), block)
            acc = None
            for xx in range(first, 4):
                rhs = db[2 * xx : 2 * xx + 2, :, :, lanes].reshape(2 * drows, wide)
                term = jnp.dot(g[xx, m, :], rhs, preferred_element_type=F32)
                acc = term if acc is None else acc + term
            s[m, :] = acc.astype(BF16)

        @pl.loop(0, steps)
        def _(i):
            m = pl.ds(al(i * block, block), block)
            acc = jnp.dot(lb[0, m, :], s[:cols, :], preferred_element_type=F32)
            acc += jnp.dot(lb[1, m, :], s[cols:, :], preferred_element_type=F32)
            t[c, m, :] = acc.astype(BF16)

        done["rs1", c] = [
            remote(t.at[c, thin(2 * y2)], rs1.at[c, 0], {"y": yp}),
            remote(t.at[c, thin(2 * y2 + 1)], rs1.at[c, 1], {"y": ym}),
        ]

    def s2(c):
        up, down = done["rs1", c]
        up.wait_recv()
        t[c, thin(2 * yp), :] = (t[c, thin(2 * yp), :].astype(F32) + rs1[c, 0].astype(F32)).astype(BF16)
        down.wait_recv()
        t[c, thin(2 * ym + 1), :] = (t[c, thin(2 * ym + 1), :].astype(F32) + rs1[c, 1].astype(F32)).astype(BF16)
        done["rs2", c] = [
            remote(t.at[c, slab(yp)], rs2.at[c, 0], {"y": yp}),
            remote(t.at[c, slab(ym)], rs2.at[c, 1], {"y": ym}),
        ]

    def s3(c):
        for copy in done["rs2", c]:
            copy.wait_recv()
        away = 1 - zl
        for dst, z in ((rsz.at[c, 0], away), (own.at[c], zl)):
            total = t[c, thin(2 * y + z), :].astype(F32)
            for side in range(2):
                total += rs2[c, side, pl.ds(al(z * part, part), part), :].astype(F32)
            dst[...] = total.astype(dst.dtype)
        done["rsz", c] = remote(rsz.at[c, 0], rsz.at[c, 1], {"zl": 1 - zl})

    def s4(c):
        done["rsz", c].wait_recv()
        irs[c][k, thin(piece), :] = (-(own[c] + rsz[c, 1].astype(F32))).astype(BF16)
        src = irs[c].at[k, thin(piece)]
        done["agz", c] = remote(src, src, {"zl": 1 - zl})
        n = counts["remote"]
        counts["remote"] += 1
        dst = iqs[c].at[k, thin(piece)]
        away = pltpu.make_async_remote_copy(
            src_ref=src, dst_ref=dst, send_sem=send.at[n], recv_sem=recv.at[n], device_id=tr_to, device_id_type=MESH
        )
        still = pltpu.make_async_copy(src, dst, recv.at[n])
        done["tr", c] = away, still

        @pl.when(jnp.logical_not(diagonal))
        def _():
            away.start()

        @pl.when(diagonal)
        def _():
            still.start()

    def s5a(c):
        done["agz", c].wait_recv()
        src = irs[c].at[k, slab(y)]
        done["agy", c] = [remote(src, src, {"y": yp}), remote(src, src, {"y": ym})]

    def s5b(c):
        away, still = done["tr", c]

        @pl.when(jnp.logical_not(diagonal))
        def _():
            away.wait_recv()

        @pl.when(diagonal)
        def _():
            still.wait()

        src = iqs[c].at[k, thin(got)]
        done["cgz", c] = remote(src, src, {"zh": 1 - zh})

    def s6a(c):
        for copy in done["agy", c]:
            copy.wait_recv()
        low, high = irs[c].at[k, thin(2 * ym)], irs[c].at[k, thin(2 * yp + 1)]
        done["agy2", c] = [remote(low, low, {"y": yp}), remote(high, high, {"y": ym})]

    def s6b(c):
        done["cgz", c].wait_recv()
        src = iqs[c].at[k, slab(bx)]
        done["cgx", c] = [remote(src, src, {"x": xp}), remote(src, src, {"x": xm})]

    def s7a(c):
        for copy in done["agy2", c]:
            copy.wait_recv()
        done["ir", c] = remote(irs[c].at[k], irs[c].at[k], {"k": 1 - k})

    def s7b(c):
        for copy in done["cgx", c]:
            copy.wait_recv()
        low, high = iqs[c].at[k, thin(2 * bxm)], iqs[c].at[k, thin(2 * bxp + 1)]
        done["cgx2", c] = [remote(low, low, {"x": xp}), remote(high, high, {"x": xm})]

    def s8(c):
        for copy in done["cgx2", c]:
            copy.wait_recv()
        src = iqs[c].at[k, pl.ds(al((1 - k) * cols, cols), cols)]
        done["iq", c] = remote(src, src, {"k": 1 - k})

    def s9(c):
        done["ir", c].wait_recv()
        done["iq", c].wait_recv()

        @pl.loop(0, steps)
        def _(i):
            m = pl.ds(al(i * block, block), block)
            acc = cb[m, :]
            for p in range(2):
                acc += lax.dot_general(
                    irs[c][p, m, :], iqs[c][p, pl.ds(al(k * cols, cols), cols), :],
                    (((1,), (1,)), ((), ())), preferred_element_type=F32,
                )
            cb[m, :] = acc

    steps_of = (relay, zwait, d1, d2, d3, d4, s1, s2, s3, s4, s5a, s5b, s6a, s6b, s7a, s7b, s8, s9)
    based = False
    added = []
    for entry in ORDER:
        step, args = steps_of[entry[0]], entry[1:]
        if step is s1 and not based:
            base()
            based = True
        if step is s9 and not added:
            c_own.wait()
        if step is s9:
            added.append(args[0])
            if len(added) == CHUNKS:
                break
        step(*args)
    done["ir", final].wait_recv()
    done["iq", final].wait_recv()
    for copy in sent + f_a:
        copy.wait_send()
    for c in range(CHUNKS):
        @pl.when(x >= c)
        def _():
            for n in range(len(group)):
                d_copy(c, n).wait_send()

        for u in range(SUB):
            for n in range(1, 3):
                for h in range(2):
                    @pl.when(when_at(c, (4 - n) % 4 if h else n))
                    def _():
                        hop(c, h, 0, u).wait_send()

            @pl.when(when_at(c, 0))
            def _():
                for h in range(2):
                    hop(c, h, 1, u).wait_send()

            @pl.when(when_at(c, 2))
            def _():
                for h in range(2):
                    across(c, h, u).wait_send()
                    hop(c, h, 1, u).wait_send()

    for c in range(CHUNKS):
        @pl.when(jnp.logical_not(diagonal))
        def _():
            done["tr", c][0].wait_send()


def last(c_ref, ir_ref, iq_ref, out_ref):
    tall, cols = out_ref.shape
    block = pl.ds(al(lax.axis_index("k") * cols, cols), cols)
    m = pl.ds(al(pl.program_id(0) * tall, tall), tall)
    total = c_ref[m, :]
    for p in range(2):
        total += lax.dot_general(
            ir_ref[p, m, :], iq_ref[p, block, :], (((1,), (1,)), ((), ())), preferred_element_type=F32
        )
    out_ref[...] = total


def solution(mesh):
    devices = mesh.devices
    split = Mesh(devices.reshape(2, 4, 2, 4, 2), AXES)

    def body(held, factor, inverses, covariance):
        rows, cols = held.shape
        fcols = factor.shape[2]
        drows, width = inverses.shape[1:]
        wide = width // CHUNKS
        part = rows // 8
        n_remote = 2 + 2 * SUB + 22 * CHUNKS
        partial_sum, left, right = pl.pallas_call(
            kernel,
            out_shape=[
                pltpu.VMEM((rows, cols), F32),
                pltpu.VMEM((2, rows, wide), BF16),
                pltpu.VMEM((2, 2 * cols, wide), BF16),
            ],
            in_specs=[pl.BlockSpec(memory_space=pltpu.HBM)] * 4,
            out_specs=[pl.BlockSpec(memory_space=pltpu.VMEM)] * 3,
            scratch_shapes=[
                pltpu.VMEM((2, rows, cols), BF16),
                pltpu.VMEM((4, 2 * cols, 2 * fcols), BF16),
                pltpu.VMEM((8, 4, drows // 4, width), BF16),
                pltpu.VMEM((2 * cols, wide), BF16),
                pltpu.VMEM((CHUNKS, rows, wide), BF16),
                pltpu.VMEM((CHUNKS, part, wide), F32),
                pltpu.VMEM((CHUNKS, 2, part, wide), BF16),
                pltpu.VMEM((CHUNKS, 2, 2 * part, wide), BF16),
                pltpu.VMEM((CHUNKS, 2, part, wide), BF16),
                pltpu.VMEM((2, CHUNKS - 1, rows, wide), BF16),
                pltpu.VMEM((2, CHUNKS - 1, rows, wide), BF16),
                pltpu.SemaphoreType.DMA((n_remote,)),
                pltpu.SemaphoreType.DMA((n_remote,)),
                pltpu.SemaphoreType.DMA((16 * SUB,)),
                pltpu.SemaphoreType.DMA((16 * SUB,)),
                pltpu.SemaphoreType.DMA((2 * SUB,)),
                pltpu.SemaphoreType.DMA((CHUNKS, 7)),
                pltpu.SemaphoreType.DMA((CHUNKS, 7)),
                pltpu.SemaphoreType.DMA((CHUNKS,)),
                pltpu.SemaphoreType.DMA((8 * SUB,)),
                pltpu.SemaphoreType.DMA((8 * SUB,)),
                pltpu.SemaphoreType.DMA((8,)),
            ],
            compiler_params=pltpu.CompilerParams(
                collective_id=0, has_side_effects=True, vmem_limit_bytes=50 * 1024 * 1024
            ),
        )(held, factor, inverses, covariance)
        tall = 256
        return pl.pallas_call(
            last,
            out_shape=jax.ShapeDtypeStruct(covariance.shape, covariance.dtype),
            grid=(rows // tall,),
            in_specs=[pl.BlockSpec(memory_space=pltpu.VMEM)] * 3,
            out_specs=pl.BlockSpec((tall, cols), lambda i: (i, 0)),
            compiler_params=pltpu.CompilerParams(vmem_limit_bytes=8 * 1024 * 1024),
        )(partial_sum, left, right)

    spec = P(("x", "zh"), ("zl", "y", "k"))
    return jax.shard_map(
        body,
        mesh=split,
        in_specs=(spec, P(None, ("zl", "y", "k"), ("x", "zh")), P(None, ("x", "zh"), None), spec),
        out_specs=spec,
        check_vma=False,
    )
```

```python
import jax
import jax.numpy as jnp
from jax import lax
from jax.experimental import pallas as pl
from jax.experimental.pallas import tpu as pltpu
from jax.sharding import Mesh
from jax.sharding import PartitionSpec as P

MESH = pl.DeviceIdType.MESH
AXES = ("zl", "x", "zh", "y", "k")
BF16 = jnp.bfloat16
F32 = jnp.float32

CHUNKS = 4
SUB = 2
LAST = 8
ORDER = (
    (0,2,0,1,1), (0,1,0,0,1), (0,0,0,1,1), (0,1,0,1,1), (0,3,0,0,1), (1,0), (0,2,0,0,1), (0,3,0,0,2), (0,3,0,1,1),
    (0,3,1,0,0), (0,3,1,0,1), (0,2,0,1,2), (0,0,0,0,1), (3,3), (1,1), (0,1,1,0,0), (0,1,0,0,2), (0,2,1,0,0),
    (0,3,1,1,0), (0,0,0,1,2), (3,1), (0,0,1,0,0), (0,2,1,1,0), (3,2), (0,1,1,0,1), (0,3,0,1,2), (0,1,1,1,0),
    (0,2,1,1,1), (0,0,1,1,0), (0,2,0,0,2), (0,1,0,1,2), (3,0), (0,1,1,1,1), (0,0,1,1,1), (0,3,1,1,1), (0,2,1,0,1),
    (4,3), (0,1,0,0,3), (0,3,1,0,2), (0,0,0,0,2), (0,1,1,0,2), (0,0,1,0,1), (0,0,1,1,2), (4,1), (0,2,0,1,3),
    (0,2,1,1,2), (4,2), (0,3,1,1,2), (5,2), (5,1), (0,0,0,0,3), (0,0,1,0,2), (0,3,0,1,3), (4,0), (0,3,1,0,3),
    (0,1,0,1,3), (0,2,1,0,2), (0,2,0,0,3), (0,3,1,1,3), (0,3,0,0,3), (5,3), (0,2,1,1,3), (0,1,1,1,2), (0,0,1,1,3),
    (0,0,0,1,3), (6,3), (0,2,1,0,3), (6,2), (0,1,1,0,3), (5,0), (0,1,1,1,3), (7,3), (6,1), (7,2), (8,3), (0,0,1,0,3),
    (7,1), (6,0), (8,2), (9,3), (8,1), (9,2), (7,0), (11,3), (10,2), (9,1), (13,3), (8,0), (11,2), (10,3), (9,0),
    (15,3), (13,2), (10,1), (11,1), (16,3), (12,2), (13,1), (10,0), (11,0), (15,2), (14,2), (12,3), (13,0), (15,1),
    (12,1), (12,0), (16,2), (14,3), (15,0), (17,2), (14,1), (16,1), (17,3), (14,0), (16,0), (17,1), (17,0),
)


def al(i, n):
    return pl.multiple_of(i, n)


def kernel(
    l_ref, f_ref, d_ref, c_ref, cb, irl_ref, iql_ref,
    lb, g, db, s, t, own, rs1, rs2, rsz, ir, iq, send, recv, send_f, recv_f, send_a, send_d, recv_d, local_d, send_x, recv_x, local,
):
    zl, x, zh, y, k = (lax.axis_index(a) for a in AXES)
    rows, cols = l_ref.shape
    _, _, fcols = f_ref.shape
    drows, width = d_ref.shape[1:]
    wide = width // CHUNKS
    part = rows // 8
    pair = 2 * part
    r = 2 * x + zh
    xp, xm = lax.rem(x + 1, 4), lax.rem(x + 3, 4)
    yp, ym, y2 = lax.rem(y + 1, 4), lax.rem(y + 3, 4), lax.rem(y + 2, 4)
    piece = 2 * y + zl

    ys, zs = 2 * lax.rem(x, 2) + zh, x // 2
    d_to, e_to = lax.rem(y - ys + 4, 4), lax.rem(zl + zs, 2)
    tr_to = {"zl": zs, "x": lax.rem(x + d_to, 4), "zh": lax.rem(zh + e_to, 2), "y": ys}
    xs, hs = 2 * zl + y // 2, lax.rem(y, 2)
    d_from, e_from = lax.rem(x - xs + 4, 4), lax.rem(zh + hs, 2)
    tr_from = {"zl": lax.rem(zl + e_from, 2), "x": xs, "zh": hs, "y": lax.rem(y + d_from, 4)}
    diagonal = jnp.logical_and(d_to == 0, e_to == 0)
    got = 2 * lax.rem(y + d_from, 4) + lax.rem(zl + e_from, 2)
    gotz = 2 * lax.rem(y + d_from, 4) + lax.rem(zl + e_from + 1, 2)
    bx = lax.rem(y + d_from, 4)
    bxp, bxm = lax.rem(bx + 1, 4), lax.rem(bx + 3, 4)

    shifts = [(dx, dz) for dx in range(4) for dz in range(2) if dx or dz]
    group = [
        {"x": lax.rem(x + dx, 4), "zh": lax.rem(zh + dz, 2), "zl": lax.rem(zl + dz, 2)} for dx, dz in shifts
    ]
    peers = group + [
        {"zh": 1 - zh},
        {"k": 1 - k}, {"zh": 1 - zh, "k": 1 - k}, {"x": xp, "k": 1 - k}, {"x": xm, "k": 1 - k},
        {"zl": 1 - zl}, {"y": yp}, {"y": ym},
    ]
    barrier = pltpu.get_barrier_semaphore()
    for peer in peers:
        pl.semaphore_signal(barrier, inc=1, device_id=peer, device_id_type=MESH)

    @pl.when(jnp.logical_not(diagonal))
    def _():
        pl.semaphore_signal(barrier, inc=1, device_id=tr_to, device_id_type=MESH)
        pl.semaphore_signal(barrier, inc=1, device_id=tr_from, device_id_type=MESH)
        pl.semaphore_wait(barrier, len(peers) + 2)

    @pl.when(diagonal)
    def _():
        pl.semaphore_wait(barrier, len(peers))

    final = [entry for entry in ORDER if entry[0] == 17][-1][1]
    irs = {c: ir.at[:, n] for n, c in enumerate(c for c in range(CHUNKS) if c != final)}
    iqs = {c: iq.at[:, n] for n, c in enumerate(c for c in range(CHUNKS) if c != final)}
    irs[final], iqs[final] = irl_ref, iql_ref
    counts = {"remote": 0, "local": 0}
    sent = []

    def remote(src, dst, device):
        n = counts["remote"]
        counts["remote"] += 1
        copy = pltpu.make_async_remote_copy(
            src_ref=src, dst_ref=dst, send_sem=send.at[n], recv_sem=recv.at[n],
            device_id=device, device_id_type=MESH,
        )
        sent.append(copy)
        copy.start()
        return copy

    def here(src, dst):
        n = counts["local"]
        counts["local"] += 1
        copy = pltpu.make_async_copy(src, dst, local.at[n])
        copy.start()
        return copy

    dpart = drows // 4

    def d_copy(c, n):
        lanes = pl.ds(c * wide, wide)
        src = d_ref.at[k, pl.ds(al(y * dpart, dpart), dpart), lanes]
        dst = db.at[r, y, :, lanes]
        if n < 0:
            return pltpu.make_async_copy(src, dst, local_d.at[c])
        return pltpu.make_async_remote_copy(
            src_ref=src, dst_ref=dst, send_sem=send_d.at[c, n], recv_sem=recv_d.at[c, n],
            device_id=group[n], device_id_type=MESH,
        )

    def d_spread(c):
        @pl.when(x >= c)
        def _():
            for n in range(-1, len(group)):
                d_copy(c, n).start()

    d_spread(CHUNKS - 1)

    sub = cols // SUB

    def rows_f(h, u):
        return pl.ds(al(h * cols + u * sub, sub), sub)

    def lanes_f(hh):
        return pl.ds(al(hh * fcols, fcols), fcols)

    def src_f(p, u):
        return f_ref.at[p, pl.ds(u * sub, sub), :]

    slots = [g.at[x, rows_f(k, u), lanes_f(zh)] for u in range(SUB)]
    f_z = [
        [
            remote(src_f(k, u), slots[u], {"zh": 1 - zh}),
            remote(src_f(1 - k, u), slots[u], {"zh": 1 - zh, "k": 1 - k}),
        ]
        for u in range(SUB)
    ]

    def hop(c, h, ab, u):
        n = ((c * 2 + h) * 2 + ab) * SUB + u
        ref = g.at[c, rows_f(h, u), lanes_f(1 - zh if ab else zh)]
        return pltpu.make_async_remote_copy(
            src_ref=ref, dst_ref=ref, send_sem=send_f.at[n], recv_sem=recv_f.at[n],
            device_id={"x": xm if h else xp}, device_id_type=MESH,
        )

    ahead = jnp.where(k == 0, xp, xm)
    f_a = []
    for u in range(SUB):
        n = (x * 2 + k) * 2 * SUB + u
        for p, device in ((k, {"x": ahead}), (1 - k, {"x": ahead, "k": 1 - k})):
            copy = pltpu.make_async_remote_copy(
                src_ref=src_f(p, u), dst_ref=slots[u], send_sem=send_a.at[len(f_a)], recv_sem=recv_f.at[n],
                device_id=device, device_id_type=MESH,
            )
            copy.start()
            f_a.append(copy)
    own_slot = g.at[x, pl.ds(al(k * cols, cols), cols), lanes_f(zh)]
    f_own = here(f_ref.at[k], own_slot)
    f_k = remote(f_ref.at[1 - k], own_slot, {"k": 1 - k})
    l_own = here(l_ref, lb.at[k])
    l_k = remote(l_ref, lb.at[k], {"k": 1 - k})
    c_own = here(c_ref, cb)
    done = {}

    def when_at(c, n):
        return lax.rem(x - c + 4, 4) == n

    def across(c, h, u):
        n = (c * 2 + h) * SUB + u
        ref = g.at[c, rows_f(h, u), lanes_f(zh)]
        return pltpu.make_async_remote_copy(
            src_ref=ref, dst_ref=ref, send_sem=send_x.at[n], recv_sem=recv_x.at[n],
            device_id={"zh": 1 - zh}, device_id_type=MESH,
        )

    def relay(c, ab, u, n):
        if ab == 0:
            for h in range(2):
                @pl.when(when_at(c, (4 - n) % 4 if h else n))
                def _():
                    copy = hop(c, h, 0, u)
                    copy.wait_recv()
                    if n < 3:
                        copy.start()
            return

        at = when_at(c, 0) if n == 0 else when_at(c, 2)
        if n == 3:
            at = jnp.logical_or(when_at(c, 1), when_at(c, 3))

        @pl.when(at)
        def _():
            for h in range(2):
                if n == 1:
                    across(c, h, u).start()
                    continue
                if n == 2:
                    across(c, h, u).wait_recv()
                if n == 3:
                    hop(c, h, 1, u).wait_recv()
                else:
                    hop(c, h, 1, u).start()

    def zwait(u):
        for copy in f_z[u]:
            copy.wait_recv()

    for c in range(CHUNKS - 2, -1, -1):
        d_spread(c)

    def dview(c, q, rows_d):
        return db.at[pl.ds(2 * c, 8 - 2 * c), q, rows_d, pl.ds(c * wide, wide)]

    def d1(c):
        pass

    def d2(c):
        @pl.when(x >= c)
        def _():
            d_copy(c, -1).wait()

        for n, (dx, _) in enumerate(shifts):
            @pl.when(lax.rem(x - dx + 4, 4) >= c)
            def _():
                d_copy(c, n).wait_recv()
        src = dview(c, y, pl.ds(0, dpart))
        done["dy", c] = [remote(src, src, {"y": yp}), remote(src, src, {"y": ym})]

    def d3(c):
        for copy in done["dy", c]:
            copy.wait_recv()
        half = dpart // 2
        low, high = dview(c, ym, pl.ds(0, half)), dview(c, yp, pl.ds(half, half))
        done["dy2", c] = [remote(low, low, {"y": yp}), remote(high, high, {"y": ym})]

    def d4(c):
        for copy in done["dy2", c]:
            copy.wait_recv()

    def base():
        f_own.wait()
        f_k.wait_recv()
        l_own.wait()
        l_k.wait_recv()

    block = 512
    steps = rows // block

    def slab(b):
        return pl.ds(al(b * pair, pair), pair)

    def thin(p):
        return pl.ds(al(p * part, part), part)

    def s1(c):
        lanes = slice(c * wide, (c + 1) * wide)
        first = c * wide // (2 * drows)

        @pl.loop(0, steps)
        def _(i):
            m = pl.ds(al(i * block, block), block)
            acc = None
            for xx in range(first, 4):
                rhs = db[2 * xx : 2 * xx + 2, :, :, lanes].reshape(2 * drows, wide)
                term = jnp.dot(g[xx, m, :], rhs, preferred_element_type=F32)
                acc = term if acc is None else acc + term
            s[m, :] = acc.astype(BF16)

        @pl.loop(0, steps)
        def _(i):
            m = pl.ds(al(i * block, block), block)
            acc = jnp.dot(lb[0, m, :], s[:cols, :], preferred_element_type=F32)
            acc += jnp.dot(lb[1, m, :], s[cols:, :], preferred_element_type=F32)
            t[c, m, :] = acc.astype(BF16)

        done["rs1", c] = [
            remote(t.at[c, thin(2 * y2)], rs1.at[c, 0], {"y": yp}),
            remote(t.at[c, thin(2 * y2 + 1)], rs1.at[c, 1], {"y": ym}),
        ]

    def s2(c):
        up, down = done["rs1", c]
        up.wait_recv()
        t[c, thin(2 * yp), :] = (t[c, thin(2 * yp), :].astype(F32) + rs1[c, 0].astype(F32)).astype(BF16)
        down.wait_recv()
        t[c, thin(2 * ym + 1), :] = (t[c, thin(2 * ym + 1), :].astype(F32) + rs1[c, 1].astype(F32)).astype(BF16)
        done["rs2", c] = [
            remote(t.at[c, slab(yp)], rs2.at[c, 0], {"y": yp}),
            remote(t.at[c, slab(ym)], rs2.at[c, 1], {"y": ym}),
        ]

    def s3(c):
        for copy in done["rs2", c]:
            copy.wait_recv()
        away = 1 - zl
        for dst, z in ((rsz.at[c, 0], away), (own.at[c], zl)):
            total = t[c, thin(2 * y + z), :].astype(F32)
            for side in range(2):
                total += rs2[c, side, pl.ds(al(z * part, part), part), :].astype(F32)
            dst[...] = total.astype(dst.dtype)
        done["rsz", c] = remote(rsz.at[c, 0], rsz.at[c, 1], {"zl": 1 - zl})

    def s4(c):
        done["rsz", c].wait_recv()
        irs[c][k, thin(piece), :] = (-(own[c] + rsz[c, 1].astype(F32))).astype(BF16)
        src = irs[c].at[k, thin(piece)]
        done["agz", c] = remote(src, src, {"zl": 1 - zl})
        n = counts["remote"]
        counts["remote"] += 1
        dst = iqs[c].at[k, thin(piece)]
        away = pltpu.make_async_remote_copy(
            src_ref=src, dst_ref=dst, send_sem=send.at[n], recv_sem=recv.at[n], device_id=tr_to, device_id_type=MESH
        )
        still = pltpu.make_async_copy(src, dst, recv.at[n])
        done["tr", c] = away, still

        @pl.when(jnp.logical_not(diagonal))
        def _():
            away.start()

        @pl.when(diagonal)
        def _():
            still.start()

    def s5a(c):
        done["agz", c].wait_recv()
        src = irs[c].at[k, slab(y)]
        done["agy", c] = [remote(src, src, {"y": yp}), remote(src, src, {"y": ym})]

    def s5b(c):
        away, still = done["tr", c]

        @pl.when(jnp.logical_not(diagonal))
        def _():
            away.wait_recv()

        @pl.when(diagonal)
        def _():
            still.wait()

        src = iqs[c].at[k, thin(got)]
        done["cgz", c] = remote(src, src, {"zh": 1 - zh})

    def s6a(c):
        for copy in done["agy", c]:
            copy.wait_recv()
        low, high = irs[c].at[k, thin(2 * ym)], irs[c].at[k, thin(2 * yp + 1)]
        done["agy2", c] = [remote(low, low, {"y": yp}), remote(high, high, {"y": ym})]

    def s6b(c):
        done["cgz", c].wait_recv()
        src = iqs[c].at[k, slab(bx)]
        done["cgx", c] = [remote(src, src, {"x": xp}), remote(src, src, {"x": xm})]

    def s7a(c):
        for copy in done["agy2", c]:
            copy.wait_recv()
        done["ir", c] = remote(irs[c].at[k], irs[c].at[k], {"k": 1 - k})

    def s7b(c):
        for copy in done["cgx", c]:
            copy.wait_recv()
        low, high = iqs[c].at[k, thin(2 * bxm)], iqs[c].at[k, thin(2 * bxp + 1)]
        done["cgx2", c] = [remote(low, low, {"x": xp}), remote(high, high, {"x": xm})]

    def s8(c):
        for copy in done["cgx2", c]:
            copy.wait_recv()
        src = iqs[c].at[k, pl.ds(al((1 - k) * cols, cols), cols)]
        done["iq", c] = remote(src, src, {"k": 1 - k})

    def s9(c):
        done["ir", c].wait_recv()
        done["iq", c].wait_recv()

        @pl.loop(0, steps)
        def _(i):
            m = pl.ds(al(i * block, block), block)
            acc = cb[m, :]
            for p in range(2):
                acc += lax.dot_general(
                    irs[c][p, m, :], iqs[c][p, pl.ds(al(k * cols, cols), cols), :],
                    (((1,), (1,)), ((), ())), preferred_element_type=F32,
                )
            cb[m, :] = acc

    steps_of = (relay, zwait, d1, d2, d3, d4, s1, s2, s3, s4, s5a, s5b, s6a, s6b, s7a, s7b, s8, s9)
    based = False
    added = []
    for entry in ORDER:
        step, args = steps_of[entry[0]], entry[1:]
        if step is s1 and not based:
            base()
            based = True
        if step is s9 and not added:
            c_own.wait()
        if step is s9:
            added.append(args[0])
            if len(added) == CHUNKS:
                break
        step(*args)
    done["ir", final].wait_recv()
    done["iq", final].wait_recv()
    for copy in sent + f_a:
        copy.wait_send()
    for c in range(CHUNKS):
        @pl.when(x >= c)
        def _():
            for n in range(len(group)):
                d_copy(c, n).wait_send()

        for u in range(SUB):
            for n in range(1, 3):
                for h in range(2):
                    @pl.when(when_at(c, (4 - n) % 4 if h else n))
                    def _():
                        hop(c, h, 0, u).wait_send()

            @pl.when(when_at(c, 0))
            def _():
                for h in range(2):
                    hop(c, h, 1, u).wait_send()

            @pl.when(when_at(c, 2))
            def _():
                for h in range(2):
                    across(c, h, u).wait_send()
                    hop(c, h, 1, u).wait_send()

    for c in range(CHUNKS):
        @pl.when(jnp.logical_not(diagonal))
        def _():
            done["tr", c][0].wait_send()


def last(c_ref, ir_ref, iq_ref, out_ref, total, sems):
    rows, cols = total.shape
    block = pl.ds(al(lax.axis_index("k") * cols, cols), cols)
    tall = rows // LAST
    copies = []
    for i in range(LAST):
        m = pl.ds(i * tall, tall)
        value = c_ref[m, :]
        for p in range(2):
            value += lax.dot_general(
                ir_ref[p, m, :], iq_ref[p, block, :], (((1,), (1,)), ((), ())), preferred_element_type=F32
            )
        total[m, :] = value
        copies.append(pltpu.make_async_copy(total.at[m], out_ref.at[m], sems.at[i]))
        copies[-1].start()
    for copy in copies:
        copy.wait()


def solution(mesh):
    devices = mesh.devices
    split = Mesh(devices.reshape(2, 4, 2, 4, 2), AXES)

    def body(held, factor, inverses, covariance):
        rows, cols = held.shape
        fcols = factor.shape[2]
        drows, width = inverses.shape[1:]
        wide = width // CHUNKS
        part = rows // 8
        n_remote = 2 + 2 * SUB + 22 * CHUNKS
        partial_sum, left, right = pl.pallas_call(
            kernel,
            out_shape=[
                pltpu.VMEM((rows, cols), F32),
                pltpu.VMEM((2, rows, wide), BF16),
                pltpu.VMEM((2, 2 * cols, wide), BF16),
            ],
            in_specs=[pl.BlockSpec(memory_space=pltpu.HBM)] * 4,
            out_specs=[pl.BlockSpec(memory_space=pltpu.VMEM)] * 3,
            scratch_shapes=[
                pltpu.VMEM((2, rows, cols), BF16),
                pltpu.VMEM((4, 2 * cols, 2 * fcols), BF16),
                pltpu.VMEM((8, 4, drows // 4, width), BF16),
                pltpu.VMEM((2 * cols, wide), BF16),
                pltpu.VMEM((CHUNKS, rows, wide), BF16),
                pltpu.VMEM((CHUNKS, part, wide), F32),
                pltpu.VMEM((CHUNKS, 2, part, wide), BF16),
                pltpu.VMEM((CHUNKS, 2, 2 * part, wide), BF16),
                pltpu.VMEM((CHUNKS, 2, part, wide), BF16),
                pltpu.VMEM((2, CHUNKS - 1, rows, wide), BF16),
                pltpu.VMEM((2, CHUNKS - 1, rows, wide), BF16),
                pltpu.SemaphoreType.DMA((n_remote,)),
                pltpu.SemaphoreType.DMA((n_remote,)),
                pltpu.SemaphoreType.DMA((16 * SUB,)),
                pltpu.SemaphoreType.DMA((16 * SUB,)),
                pltpu.SemaphoreType.DMA((2 * SUB,)),
                pltpu.SemaphoreType.DMA((CHUNKS, 7)),
                pltpu.SemaphoreType.DMA((CHUNKS, 7)),
                pltpu.SemaphoreType.DMA((CHUNKS,)),
                pltpu.SemaphoreType.DMA((8 * SUB,)),
                pltpu.SemaphoreType.DMA((8 * SUB,)),
                pltpu.SemaphoreType.DMA((8,)),
            ],
            compiler_params=pltpu.CompilerParams(
                collective_id=0, has_side_effects=True, vmem_limit_bytes=50 * 1024 * 1024
            ),
        )(held, factor, inverses, covariance)
        return pl.pallas_call(
            last,
            out_shape=jax.ShapeDtypeStruct(covariance.shape, covariance.dtype),
            in_specs=[pl.BlockSpec(memory_space=pltpu.VMEM)] * 3,
            out_specs=pl.BlockSpec(memory_space=pltpu.HBM),
            scratch_shapes=[pltpu.VMEM((rows, cols), F32), pltpu.SemaphoreType.DMA((LAST,))],
            compiler_params=pltpu.CompilerParams(vmem_limit_bytes=6 * 1024 * 1024),
        )(partial_sum, left, right)

    spec = P(("x", "zh"), ("zl", "y", "k"))
    return jax.shard_map(
        body,
        mesh=split,
        in_specs=(spec, P(None, ("zl", "y", "k"), ("x", "zh")), P(None, ("x", "zh"), None), spec),
        out_specs=spec,
        check_vma=False,
    )
```

```python
import jax
import jax.numpy as jnp
from jax import lax
from jax.experimental import pallas as pl
from jax.experimental.pallas import tpu as pltpu
from jax.sharding import Mesh
from jax.sharding import PartitionSpec as P

MESH = pl.DeviceIdType.MESH
AXES = ("zl", "x", "zh", "y", "k")
BF16 = jnp.bfloat16
F32 = jnp.float32

CHUNKS = 4
SUB = 2
LAST = 8
ORDER = (
    (0,2,0,1,1), (0,1,0,0,1), (0,0,0,1,1), (0,1,0,1,1), (0,3,0,0,1), (1,0), (0,2,0,0,1), (0,3,0,0,2), (0,3,0,1,1),
    (0,3,1,0,0), (0,3,1,0,1), (0,2,0,1,2), (0,0,0,0,1), (3,3), (1,1), (0,1,1,0,0), (0,1,0,0,2), (0,2,1,0,0),
    (0,3,1,1,0), (0,0,0,1,2), (3,1), (0,0,1,0,0), (0,2,1,1,0), (3,2), (0,1,1,0,1), (0,3,0,1,2), (0,1,1,1,0),
    (0,2,1,1,1), (0,0,1,1,0), (0,2,0,0,2), (0,1,0,1,2), (3,0), (0,1,1,1,1), (0,0,1,1,1), (0,3,1,1,1), (0,2,1,0,1),
    (4,3), (0,1,0,0,3), (0,3,1,0,2), (0,0,0,0,2), (0,1,1,0,2), (0,0,1,0,1), (0,0,1,1,2), (4,1), (0,2,0,1,3),
    (0,2,1,1,2), (4,2), (0,3,1,1,2), (5,2), (5,1), (0,0,0,0,3), (0,0,1,0,2), (0,3,0,1,3), (4,0), (0,3,1,0,3),
    (0,1,0,1,3), (0,2,1,0,2), (0,2,0,0,3), (0,3,1,1,3), (0,3,0,0,3), (5,3), (0,2,1,1,3), (0,1,1,1,2), (0,0,1,1,3),
    (0,0,0,1,3), (6,3), (0,2,1,0,3), (6,2), (0,1,1,0,3), (5,0), (0,1,1,1,3), (7,3), (6,1), (7,2), (8,3), (0,0,1,0,3),
    (7,1), (6,0), (8,2), (9,3), (8,1), (9,2), (7,0), (11,3), (10,2), (9,1), (13,3), (8,0), (11,2), (10,3), (9,0),
    (15,3), (13,2), (10,1), (11,1), (16,3), (12,2), (13,1), (10,0), (11,0), (15,2), (14,2), (12,3), (13,0), (15,1),
    (12,1), (12,0), (16,2), (14,3), (15,0), (17,2), (14,1), (16,1), (17,3), (14,0), (16,0), (17,1), (17,0),
)


def al(i, n):
    return pl.multiple_of(i, n)


def kernel(
    l_ref, f_ref, d_ref, c_ref, cb, irl_ref, iql_ref,
    lb, g, db, s, t, own, rs1, rs2, rsz, ir, iq, send, recv, send_f, recv_f, send_a, send_d, recv_d, local_d, send_x, recv_x, local,
):
    zl, x, zh, y, k = (lax.axis_index(a) for a in AXES)
    rows, cols = l_ref.shape
    _, _, fcols = f_ref.shape
    drows, width = d_ref.shape[1:]
    wide = width // CHUNKS
    part = rows // 8
    pair = 2 * part
    r = 2 * x + zh
    xp, xm = lax.rem(x + 1, 4), lax.rem(x + 3, 4)
    yp, ym, y2 = lax.rem(y + 1, 4), lax.rem(y + 3, 4), lax.rem(y + 2, 4)
    piece = 2 * y + zl

    ys, zs = 2 * lax.rem(x, 2) + zh, x // 2
    d_to, e_to = lax.rem(y - ys + 4, 4), lax.rem(zl + zs, 2)
    tr_to = {"zl": zs, "x": lax.rem(x + d_to, 4), "zh": lax.rem(zh + e_to, 2), "y": ys}
    xs, hs = 2 * zl + y // 2, lax.rem(y, 2)
    d_from, e_from = lax.rem(x - xs + 4, 4), lax.rem(zh + hs, 2)
    tr_from = {"zl": lax.rem(zl + e_from, 2), "x": xs, "zh": hs, "y": lax.rem(y + d_from, 4)}
    diagonal = jnp.logical_and(d_to == 0, e_to == 0)
    got = 2 * lax.rem(y + d_from, 4) + lax.rem(zl + e_from, 2)
    gotz = 2 * lax.rem(y + d_from, 4) + lax.rem(zl + e_from + 1, 2)
    bx = lax.rem(y + d_from, 4)
    bxp, bxm = lax.rem(bx + 1, 4), lax.rem(bx + 3, 4)

    shifts = [(dx, dz) for dx in range(4) for dz in range(2) if dx or dz]
    group = [
        {"x": lax.rem(x + dx, 4), "zh": lax.rem(zh + dz, 2), "zl": lax.rem(zl + dz, 2)} for dx, dz in shifts
    ]
    peers = group + [
        {"zh": 1 - zh},
        {"k": 1 - k}, {"zh": 1 - zh, "k": 1 - k}, {"x": xp, "k": 1 - k}, {"x": xm, "k": 1 - k},
        {"zl": 1 - zl}, {"y": yp}, {"y": ym},
    ]
    barrier = pltpu.get_barrier_semaphore()
    for peer in peers:
        pl.semaphore_signal(barrier, inc=1, device_id=peer, device_id_type=MESH)

    @pl.when(jnp.logical_not(diagonal))
    def _():
        pl.semaphore_signal(barrier, inc=1, device_id=tr_to, device_id_type=MESH)
        pl.semaphore_signal(barrier, inc=1, device_id=tr_from, device_id_type=MESH)
        pl.semaphore_wait(barrier, len(peers) + 2)

    @pl.when(diagonal)
    def _():
        pl.semaphore_wait(barrier, len(peers))

    final = [entry for entry in ORDER if entry[0] == 17][-1][1]
    irs = {c: ir.at[:, n] for n, c in enumerate(c for c in range(CHUNKS) if c != final)}
    iqs = {c: iq.at[:, n] for n, c in enumerate(c for c in range(CHUNKS) if c != final)}
    irs[final], iqs[final] = irl_ref, iql_ref
    counts = {"remote": 0, "local": 0}
    sent = []

    def remote(src, dst, device):
        n = counts["remote"]
        counts["remote"] += 1
        copy = pltpu.make_async_remote_copy(
            src_ref=src, dst_ref=dst, send_sem=send.at[n], recv_sem=recv.at[n],
            device_id=device, device_id_type=MESH,
        )
        sent.append(copy)
        copy.start()
        return copy

    def here(src, dst):
        n = counts["local"]
        counts["local"] += 1
        copy = pltpu.make_async_copy(src, dst, local.at[n])
        copy.start()
        return copy

    dpart = drows // 4

    def d_copy(c, n):
        lanes = pl.ds(c * wide, wide)
        src = d_ref.at[k, pl.ds(al(y * dpart, dpart), dpart), lanes]
        dst = db.at[r, y, :, lanes]
        if n < 0:
            return pltpu.make_async_copy(src, dst, local_d.at[c])
        return pltpu.make_async_remote_copy(
            src_ref=src, dst_ref=dst, send_sem=send_d.at[c, n], recv_sem=recv_d.at[c, n],
            device_id=group[n], device_id_type=MESH,
        )

    def d_spread(c):
        @pl.when(x >= c)
        def _():
            for n in range(-1, len(group)):
                d_copy(c, n).start()

    d_spread(CHUNKS - 1)

    sub = cols // SUB

    def rows_f(h, u):
        return pl.ds(al(h * cols + u * sub, sub), sub)

    def lanes_f(hh):
        return pl.ds(al(hh * fcols, fcols), fcols)

    def src_f(p, u):
        return f_ref.at[p, pl.ds(u * sub, sub), :]

    slots = [g.at[x, rows_f(k, u), lanes_f(zh)] for u in range(SUB)]
    f_z = [
        [
            remote(src_f(k, u), slots[u], {"zh": 1 - zh}),
            remote(src_f(1 - k, u), slots[u], {"zh": 1 - zh, "k": 1 - k}),
        ]
        for u in range(SUB)
    ]

    def hop(c, h, ab, u):
        n = ((c * 2 + h) * 2 + ab) * SUB + u
        ref = g.at[c, rows_f(h, u), lanes_f(1 - zh if ab else zh)]
        return pltpu.make_async_remote_copy(
            src_ref=ref, dst_ref=ref, send_sem=send_f.at[n], recv_sem=recv_f.at[n],
            device_id={"x": xm if h else xp}, device_id_type=MESH,
        )

    ahead = jnp.where(k == 0, xp, xm)
    f_a = []
    for u in range(SUB):
        n = (x * 2 + k) * 2 * SUB + u
        for p, device in ((k, {"x": ahead}), (1 - k, {"x": ahead, "k": 1 - k})):
            copy = pltpu.make_async_remote_copy(
                src_ref=src_f(p, u), dst_ref=slots[u], send_sem=send_a.at[len(f_a)], recv_sem=recv_f.at[n],
                device_id=device, device_id_type=MESH,
            )
            copy.start()
            f_a.append(copy)
    own_slot = g.at[x, pl.ds(al(k * cols, cols), cols), lanes_f(zh)]
    f_own = here(f_ref.at[k], own_slot)
    f_k = remote(f_ref.at[1 - k], own_slot, {"k": 1 - k})
    l_own = here(l_ref, lb.at[k])
    l_k = remote(l_ref, lb.at[k], {"k": 1 - k})
    c_own = here(c_ref, cb)
    done = {}

    def when_at(c, n):
        return lax.rem(x - c + 4, 4) == n

    def across(c, h, u):
        n = (c * 2 + h) * SUB + u
        ref = g.at[c, rows_f(h, u), lanes_f(zh)]
        return pltpu.make_async_remote_copy(
            src_ref=ref, dst_ref=ref, send_sem=send_x.at[n], recv_sem=recv_x.at[n],
            device_id={"zh": 1 - zh}, device_id_type=MESH,
        )

    def relay(c, ab, u, n):
        if ab == 0:
            for h in range(2):
                @pl.when(when_at(c, (4 - n) % 4 if h else n))
                def _():
                    copy = hop(c, h, 0, u)
                    copy.wait_recv()
                    if n < 3:
                        copy.start()
            return

        at = when_at(c, 0) if n == 0 else when_at(c, 2)
        if n == 3:
            at = jnp.logical_or(when_at(c, 1), when_at(c, 3))

        @pl.when(at)
        def _():
            for h in range(2):
                if n == 1:
                    across(c, h, u).start()
                    continue
                if n == 2:
                    across(c, h, u).wait_recv()
                if n == 3:
                    hop(c, h, 1, u).wait_recv()
                else:
                    hop(c, h, 1, u).start()

    def zwait(u):
        for copy in f_z[u]:
            copy.wait_recv()

    for c in range(CHUNKS - 2, -1, -1):
        d_spread(c)

    def dview(c, q, rows_d):
        return db.at[pl.ds(2 * c, 8 - 2 * c), q, rows_d, pl.ds(c * wide, wide)]

    def d1(c):
        pass

    def d2(c):
        @pl.when(x >= c)
        def _():
            d_copy(c, -1).wait()

        for n, (dx, _) in enumerate(shifts):
            @pl.when(lax.rem(x - dx + 4, 4) >= c)
            def _():
                d_copy(c, n).wait_recv()
        src = dview(c, y, pl.ds(0, dpart))
        done["dy", c] = [remote(src, src, {"y": yp}), remote(src, src, {"y": ym})]

    def d3(c):
        for copy in done["dy", c]:
            copy.wait_recv()
        half = dpart // 2
        low, high = dview(c, ym, pl.ds(0, half)), dview(c, yp, pl.ds(half, half))
        done["dy2", c] = [remote(low, low, {"y": yp}), remote(high, high, {"y": ym})]

    def d4(c):
        for copy in done["dy2", c]:
            copy.wait_recv()

    def base():
        f_own.wait()
        f_k.wait_recv()
        l_own.wait()
        l_k.wait_recv()

    block = 512
    steps = rows // block

    def slab(b):
        return pl.ds(al(b * pair, pair), pair)

    def thin(p):
        return pl.ds(al(p * part, part), part)

    def s1(c):
        lanes = slice(c * wide, (c + 1) * wide)
        first = c * wide // (2 * drows)

        @pl.loop(0, steps)
        def _(i):
            m = pl.ds(al(i * block, block), block)
            acc = None
            for xx in range(first, 4):
                rhs = db[2 * xx : 2 * xx + 2, :, :, lanes].reshape(2 * drows, wide)
                term = jnp.dot(g[xx, m, :], rhs, preferred_element_type=F32)
                acc = term if acc is None else acc + term
            s[m, :] = acc.astype(BF16)

        @pl.loop(0, steps)
        def _(i):
            m = pl.ds(al(i * block, block), block)
            acc = jnp.dot(lb[0, m, :], s[:cols, :], preferred_element_type=F32)
            acc += jnp.dot(lb[1, m, :], s[cols:, :], preferred_element_type=F32)
            t[c, m, :] = acc.astype(BF16)

        done["rs1", c] = [
            remote(t.at[c, thin(2 * y2)], rs1.at[c, 0], {"y": yp}),
            remote(t.at[c, thin(2 * y2 + 1)], rs1.at[c, 1], {"y": ym}),
        ]

    def s2(c):
        up, down = done["rs1", c]
        up.wait_recv()
        t[c, thin(2 * yp), :] = (t[c, thin(2 * yp), :].astype(F32) + rs1[c, 0].astype(F32)).astype(BF16)
        down.wait_recv()
        t[c, thin(2 * ym + 1), :] = (t[c, thin(2 * ym + 1), :].astype(F32) + rs1[c, 1].astype(F32)).astype(BF16)
        done["rs2", c] = [
            remote(t.at[c, slab(yp)], rs2.at[c, 0], {"y": yp}),
            remote(t.at[c, slab(ym)], rs2.at[c, 1], {"y": ym}),
        ]

    def s3(c):
        for copy in done["rs2", c]:
            copy.wait_recv()
        away = 1 - zl
        for dst, z in ((rsz.at[c, 0], away), (own.at[c], zl)):
            total = t[c, thin(2 * y + z), :].astype(F32)
            for side in range(2):
                total += rs2[c, side, pl.ds(al(z * part, part), part), :].astype(F32)
            dst[...] = total.astype(dst.dtype)
        done["rsz", c] = remote(rsz.at[c, 0], rsz.at[c, 1], {"zl": 1 - zl})

    def s4(c):
        done["rsz", c].wait_recv()
        irs[c][k, thin(piece), :] = (-(own[c] + rsz[c, 1].astype(F32))).astype(BF16)
        src = irs[c].at[k, thin(piece)]
        done["agz", c] = remote(src, src, {"zl": 1 - zl})
        n = counts["remote"]
        counts["remote"] += 1
        dst = iqs[c].at[k, thin(piece)]
        away = pltpu.make_async_remote_copy(
            src_ref=src, dst_ref=dst, send_sem=send.at[n], recv_sem=recv.at[n], device_id=tr_to, device_id_type=MESH
        )
        still = pltpu.make_async_copy(src, dst, recv.at[n])
        done["tr", c] = away, still

        @pl.when(jnp.logical_not(diagonal))
        def _():
            away.start()

        @pl.when(diagonal)
        def _():
            still.start()

    def s5a(c):
        done["agz", c].wait_recv()
        src = irs[c].at[k, slab(y)]
        done["agy", c] = [remote(src, src, {"y": yp}), remote(src, src, {"y": ym})]

    def s5b(c):
        away, still = done["tr", c]

        @pl.when(jnp.logical_not(diagonal))
        def _():
            away.wait_recv()

        @pl.when(diagonal)
        def _():
            still.wait()

        src = iqs[c].at[k, thin(got)]
        done["cgz", c] = remote(src, src, {"zh": 1 - zh})

    def share(c, b):
        src = irs[c].at[k, slab(b)]
        done.setdefault(("ir", c), []).append(remote(src, src, {"k": 1 - k}))

    def s6a(c):
        for copy in done["agy", c]:
            copy.wait_recv()
        for b in (y, yp, ym):
            share(c, b)
        low, high = irs[c].at[k, thin(2 * ym)], irs[c].at[k, thin(2 * yp + 1)]
        done["agy2", c] = [remote(low, low, {"y": yp}), remote(high, high, {"y": ym})]

    def s6b(c):
        done["cgz", c].wait_recv()
        src = iqs[c].at[k, slab(bx)]
        done["cgx", c] = [remote(src, src, {"x": xp}), remote(src, src, {"x": xm})]

    def s7a(c):
        for copy in done["agy2", c]:
            copy.wait_recv()
        share(c, y2)

    def s7b(c):
        for copy in done["cgx", c]:
            copy.wait_recv()
        low, high = iqs[c].at[k, thin(2 * bxm)], iqs[c].at[k, thin(2 * bxp + 1)]
        done["cgx2", c] = [remote(low, low, {"x": xp}), remote(high, high, {"x": xm})]

    def s8(c):
        for copy in done["cgx2", c]:
            copy.wait_recv()
        src = iqs[c].at[k, pl.ds(al((1 - k) * cols, cols), cols)]
        done["iq", c] = remote(src, src, {"k": 1 - k})

    def s9(c):
        for copy in done["ir", c]:
            copy.wait_recv()
        done["iq", c].wait_recv()

        @pl.loop(0, steps)
        def _(i):
            m = pl.ds(al(i * block, block), block)
            acc = cb[m, :]
            for p in range(2):
                acc += lax.dot_general(
                    irs[c][p, m, :], iqs[c][p, pl.ds(al(k * cols, cols), cols), :],
                    (((1,), (1,)), ((), ())), preferred_element_type=F32,
                )
            cb[m, :] = acc

    steps_of = (relay, zwait, d1, d2, d3, d4, s1, s2, s3, s4, s5a, s5b, s6a, s6b, s7a, s7b, s8, s9)
    based = False
    added = []
    for entry in ORDER:
        step, args = steps_of[entry[0]], entry[1:]
        if step is s1 and not based:
            base()
            based = True
        if step is s9 and not added:
            c_own.wait()
        if step is s9:
            added.append(args[0])
            if len(added) == CHUNKS:
                break
        step(*args)
    for copy in done["ir", final]:
        copy.wait_recv()
    done["iq", final].wait_recv()
    for copy in sent + f_a:
        copy.wait_send()
    for c in range(CHUNKS):
        @pl.when(x >= c)
        def _():
            for n in range(len(group)):
                d_copy(c, n).wait_send()

        for u in range(SUB):
            for n in range(1, 3):
                for h in range(2):
                    @pl.when(when_at(c, (4 - n) % 4 if h else n))
                    def _():
                        hop(c, h, 0, u).wait_send()

            @pl.when(when_at(c, 0))
            def _():
                for h in range(2):
                    hop(c, h, 1, u).wait_send()

            @pl.when(when_at(c, 2))
            def _():
                for h in range(2):
                    across(c, h, u).wait_send()
                    hop(c, h, 1, u).wait_send()

    for c in range(CHUNKS):
        @pl.when(jnp.logical_not(diagonal))
        def _():
            done["tr", c][0].wait_send()


def last(c_ref, ir_ref, iq_ref, out_ref, total, sems):
    rows, cols = total.shape
    block = pl.ds(al(lax.axis_index("k") * cols, cols), cols)
    tall = rows // LAST
    copies = []
    for i in range(LAST):
        m = pl.ds(i * tall, tall)
        value = c_ref[m, :]
        for p in range(2):
            value += lax.dot_general(
                ir_ref[p, m, :], iq_ref[p, block, :], (((1,), (1,)), ((), ())), preferred_element_type=F32
            )
        total[m, :] = value
        copies.append(pltpu.make_async_copy(total.at[m], out_ref.at[m], sems.at[i]))
        copies[-1].start()
    for copy in copies:
        copy.wait()


def solution(mesh):
    devices = mesh.devices
    split = Mesh(devices.reshape(2, 4, 2, 4, 2), AXES)

    def body(held, factor, inverses, covariance):
        rows, cols = held.shape
        fcols = factor.shape[2]
        drows, width = inverses.shape[1:]
        wide = width // CHUNKS
        part = rows // 8
        n_remote = 2 + 2 * SUB + 25 * CHUNKS
        partial_sum, left, right = pl.pallas_call(
            kernel,
            out_shape=[
                pltpu.VMEM((rows, cols), F32),
                pltpu.VMEM((2, rows, wide), BF16),
                pltpu.VMEM((2, 2 * cols, wide), BF16),
            ],
            in_specs=[pl.BlockSpec(memory_space=pltpu.HBM)] * 4,
            out_specs=[pl.BlockSpec(memory_space=pltpu.VMEM)] * 3,
            scratch_shapes=[
                pltpu.VMEM((2, rows, cols), BF16),
                pltpu.VMEM((4, 2 * cols, 2 * fcols), BF16),
                pltpu.VMEM((8, 4, drows // 4, width), BF16),
                pltpu.VMEM((2 * cols, wide), BF16),
                pltpu.VMEM((CHUNKS, rows, wide), BF16),
                pltpu.VMEM((CHUNKS, part, wide), F32),
                pltpu.VMEM((CHUNKS, 2, part, wide), BF16),
                pltpu.VMEM((CHUNKS, 2, 2 * part, wide), BF16),
                pltpu.VMEM((CHUNKS, 2, part, wide), BF16),
                pltpu.VMEM((2, CHUNKS - 1, rows, wide), BF16),
                pltpu.VMEM((2, CHUNKS - 1, rows, wide), BF16),
                pltpu.SemaphoreType.DMA((n_remote,)),
                pltpu.SemaphoreType.DMA((n_remote,)),
                pltpu.SemaphoreType.DMA((16 * SUB,)),
                pltpu.SemaphoreType.DMA((16 * SUB,)),
                pltpu.SemaphoreType.DMA((2 * SUB,)),
                pltpu.SemaphoreType.DMA((CHUNKS, 7)),
                pltpu.SemaphoreType.DMA((CHUNKS, 7)),
                pltpu.SemaphoreType.DMA((CHUNKS,)),
                pltpu.SemaphoreType.DMA((8 * SUB,)),
                pltpu.SemaphoreType.DMA((8 * SUB,)),
                pltpu.SemaphoreType.DMA((8,)),
            ],
            compiler_params=pltpu.CompilerParams(
                collective_id=0, has_side_effects=True, vmem_limit_bytes=50 * 1024 * 1024
            ),
        )(held, factor, inverses, covariance)
        return pl.pallas_call(
            last,
            out_shape=jax.ShapeDtypeStruct(covariance.shape, covariance.dtype),
            in_specs=[pl.BlockSpec(memory_space=pltpu.VMEM)] * 3,
            out_specs=pl.BlockSpec(memory_space=pltpu.HBM),
            scratch_shapes=[pltpu.VMEM((rows, cols), F32), pltpu.SemaphoreType.DMA((LAST,))],
            compiler_params=pltpu.CompilerParams(vmem_limit_bytes=6 * 1024 * 1024),
        )(partial_sum, left, right)

    spec = P(("x", "zh"), ("zl", "y", "k"))
    return jax.shard_map(
        body,
        mesh=split,
        in_specs=(spec, P(None, ("zl", "y", "k"), ("x", "zh")), P(None, ("x", "zh"), None), spec),
        out_specs=spec,
        check_vma=False,
    )
```
